128 devices in a mesh: ty: 4 (over y), tx: 32 (over x, z, core).
Axes of the slice: x: 4, y: 4, z: 4, core: 2. Of those that a mesh axis runs over, the one named last changes fastest.
Arguments:
- velocity_start: float32 [2, 10, 128, 8192], P(None, None, 'ty', 'tx'), may hold values from -4 to 4
- stiffness: float32 [10, 128, 8192], P(None, 'ty', 'tx'), may hold values from 0.3 to 3
- beta: float32 [128, 8192], P('ty', 'tx'), may hold values from 0.1 to 10
- ice_mask: int32 [128, 8192], P('ty', 'tx'), may hold values 0 or 1
- thickness: float32 [128, 8192], P('ty', 'tx'), may hold values from 0.5 to 2
- bed: float32 [128, 8192], P('ty', 'tx'), may hold values from -18 to 18
- land_smb: float32 [10, 65536], P(None, ('ty', 'tx')), may hold values from -6 to 6
- elev_class: int32 [128, 8192], P('ty', 'tx'), may hold values from 0 to 9
- correlation_cols: int32 [4, 128, 8192], P(None, 'ty', 'tx'), may hold values from 0 to 65535
- correlation_weights: float32 [4, 128, 8192], P(None, 'ty', 'tx'), may hold values from 0.1 to 1
Outputs:
- velocity: float32 [2, 10, 128, 8192], P(None, None, 'ty', 'tx')
- surface: float32 [128, 8192], P('ty', 'tx')
- land_surface: float32 [10, 65536], P(None, ('ty', 'tx'))
The draws below stay inside these ranges and needn't reach their ends.
All inputs are finite; a program needn't handle non-finite values. No bound on the sum of `ice_mask` on one device may be relied on, other than what follows from the above.
Results may differ from the reference program's by a relative error of at most 0.0001.
Values sent between devices are 32-bit elements; how exact they have to be, the bound alone decides.
A program may use at most 64 MiB of HBM per device.

```python
import math
import jax
import jax.numpy as jnp

LEV = 10
CLASSES = 10
OVL = 4
PICARD = 1
KRYLOV = 4
NX = 128
NY = 8192
LAND = 65536


def with_ends(values, rng, least, largest):
    spot = [jax.random.randint(jax.random.fold_in(rng, axis), (), 0, length) for axis, length in enumerate(values.shape)]
    widest = values.shape.index(max(values.shape))
    next_to = spot[:widest] + [(spot[widest] + 1) % values.shape[widest]] + spot[widest + 1:]
    return values.at[tuple(spot)].set(least).at[tuple(next_to)].set(largest)


def shard_levels(key, shape, cuts, smallest, high):
    loudness = 1.0
    for dim, shards_of in cuts:
        heights = jax.random.uniform(jax.random.fold_in(jax.random.fold_in(key, 6), dim), (shards_of,), jnp.float32, smallest / len(cuts), high / len(cuts))
        loudness = loudness * jnp.repeat(jnp.exp(heights), shape[dim] // shards_of).reshape((-1,) + (1,) * (len(shape) - 1 - dim))
    return loudness


def normal_values(stream_key, extent, width, bound, shards=(), kind=jnp.bfloat16):
    entries = width * jax.random.normal(stream_key, extent, jnp.float32)
    if shards:
        entries = entries * shard_levels(stream_key, extent, shards, -0.22, 0.18)
    return jnp.clip(entries, -bound, bound).astype(kind)


def setup_inputs(seed: int = 0) -> dict:
    splits = jax.random.split(jax.random.key(seed), 11)
    return {
        "velocity_start": normal_values(splits[0], (2, LEV, NX, NY), 0.5, 4.0, ((2, 4), (3, 32)), jnp.float32),
        "stiffness": jnp.clip(jnp.exp(math.log(3.0) - 2.3025851 * jax.random.uniform(splits[1], (LEV, NX, NY), jnp.float32) ** shard_levels(splits[1], (LEV, NX, NY), ((1, 4), (2, 32)), -0.2, 0.2)), 0.3, 3.0),
        "beta": jnp.clip(jnp.exp(math.log(10.0) - 4.6051702 * jax.random.uniform(splits[2], (NX, NY), jnp.float32) ** shard_levels(splits[2], (NX, NY), ((0, 4), (1, 32)), -0.2, 0.2)), 0.1, 10.0),
        "ice_mask": with_ends((jax.random.randint(splits[3], (NX, NY), 0, 4) < 3).astype(jnp.int32), jax.random.fold_in(splits[3], 1), 0, 1),
        "thickness": jnp.clip(0.5 + 1.5 * jax.random.uniform(splits[4], (NX, NY), jnp.float32) ** shard_levels(splits[4], (NX, NY), ((0, 4), (1, 32)), -0.2, 0.2), 0.5, 2.0),
        "bed": normal_values(splits[5], (NX, NY), 3.0, 18.0, ((0, 4), (1, 32)), jnp.float32),
        "land_smb": normal_values(splits[6], (CLASSES, LAND), 1.0, 6.0, ((1, 128),), jnp.float32),
        "elev_class": with_ends(jax.random.randint(splits[7], (NX, NY), 0, CLASSES), jax.random.fold_in(splits[7], 1), 0, CLASSES - 1).astype(jnp.int32),
        "correlation_cols": with_ends(jax.random.randint(splits[8], (OVL, NX, NY), 0, LAND), jax.random.fold_in(splits[8], 1), 0, LAND - 1).astype(jnp.int32),
        "correlation_weights": jnp.clip(0.1 + 0.9 * jax.random.uniform(splits[9], (OVL, NX, NY), jnp.float32) ** shard_levels(splits[9], (OVL, NX, NY), ((1, 4), (2, 32)), -0.2, 0.2), 0.1, 1.0),
    }


eps_strain = 0.1
vert_coupling = 2.0
time_step = 0.5


def pad_grid(field):
    widths = [(0, 0)] * (field.ndim - 2) + [(1, 1), (1, 1)]
    return jnp.pad(field, widths)


def strain_viscosity(padded, stiffness):
    flow_x = padded[0]
    flow_y = padded[1]
    grad_xx = 0.5 * (flow_x[:, 2:, 1:-1] - flow_x[:, :-2, 1:-1])
    grad_yy = 0.5 * (flow_y[:, 1:-1, 2:] - flow_y[:, 1:-1, :-2])
    grad_xy = 0.5 * (flow_x[:, 1:-1, 2:] - flow_x[:, 1:-1, :-2])
    grad_yx = 0.5 * (flow_y[:, 2:, 1:-1] - flow_y[:, :-2, 1:-1])
    inner_x = flow_x[:, 1:-1, 1:-1]
    inner_y = flow_y[:, 1:-1, 1:-1]
    shear_x = jnp.concatenate([inner_x[1:] - inner_x[:-1], jnp.zeros_like(inner_x[:1])], axis=0)
    shear_y = jnp.concatenate([inner_y[1:] - inner_y[:-1], jnp.zeros_like(inner_y[:1])], axis=0)
    rate = grad_xx * grad_xx + grad_yy * grad_yy + grad_xx * grad_yy
    rate = rate + 0.25 * (grad_xy + grad_yx) ** 2 + 0.25 * (shear_x * shear_x + shear_y * shear_y)
    return stiffness * (eps_strain + rate) ** (-1.0 / 3.0)


def face_weights(padded_mu):
    center = padded_mu[:, 1:-1, 1:-1]
    x_plus = 0.5 * (center + padded_mu[:, 2:, 1:-1])
    x_minus = 0.5 * (center + padded_mu[:, :-2, 1:-1])
    y_plus = 0.5 * (center + padded_mu[:, 1:-1, 2:])
    y_minus = 0.5 * (center + padded_mu[:, 1:-1, :-2])
    z_face = 0.5 * (center[1:] + center[:-1])
    zeros_layer = jnp.zeros_like(center[:1])
    z_plus = jnp.concatenate([z_face, zeros_layer], axis=0)
    z_minus = jnp.concatenate([zeros_layer, z_face], axis=0)
    return (x_plus, x_minus, y_plus, y_minus, z_plus, z_minus)


def stokes_apply(padded, faces, beta):
    x_plus, x_minus, y_plus, y_minus, z_plus, z_minus = faces
    center = padded[:, :, 1:-1, 1:-1]
    lateral_x = jnp.array([4.0, 1.0], dtype=jnp.float32).reshape(2, 1, 1, 1)
    lateral_y = jnp.array([1.0, 4.0], dtype=jnp.float32).reshape(2, 1, 1, 1)
    term_x = lateral_x * (x_plus * (center - padded[:, :, 2:, 1:-1]) + x_minus * (center - padded[:, :, :-2, 1:-1]))
    term_y = lateral_y * (y_plus * (center - padded[:, :, 1:-1, 2:]) + y_minus * (center - padded[:, :, 1:-1, :-2]))
    zeros_level = jnp.zeros_like(center[:, :1])
    above = jnp.concatenate([center[:, 1:], zeros_level], axis=1)
    below = jnp.concatenate([zeros_level, center[:, :-1]], axis=1)
    term_z = vert_coupling * (z_plus * (center - above) + z_minus * (center - below))
    bottom = (jnp.arange(center.shape[1]) == 0).astype(jnp.float32).reshape(1, -1, 1, 1)
    return term_x + term_y + term_z + bottom * beta * center


def reference(velocity_start, stiffness, beta, ice_mask, thickness, bed, land_smb, elev_class, correlation_cols, correlation_weights):
    mask = ice_mask.astype(jnp.float32)
    surface_old = bed + thickness
    padded_s = pad_grid(surface_old)
    slope_x = 0.5 * (padded_s[2:, 1:-1] - padded_s[:-2, 1:-1])
    slope_y = 0.5 * (padded_s[1:-1, 2:] - padded_s[1:-1, :-2])
    drive = -(mask * thickness) * jnp.stack([slope_x, slope_y])
    rhs = drive[:, None] * jnp.ones((1, LEV, 1, 1), jnp.float32)
    velocity = velocity_start
    for sweep in range(PICARD):
        visc = strain_viscosity(pad_grid(velocity), stiffness)
        faces = face_weights(pad_grid(visc))

        def operator(field):
            return mask * stokes_apply(pad_grid(mask * field), faces, beta) + (1.0 - mask) * field

        residual = rhs - operator(velocity)
        direction = residual
        norm_now = jnp.sum(residual * residual)
        for inner in range(KRYLOV):
            image = operator(direction)
            step_size = norm_now / jnp.sum(direction * image)
            velocity = velocity + step_size * direction
            residual = residual - step_size * image
            norm_next = jnp.sum(residual * residual)
            direction = residual + (norm_next / norm_now) * direction
            norm_now = norm_next
    mean_flow = jnp.mean(velocity, axis=1)
    padded_f = pad_grid(thickness * mean_flow)
    spread = 0.5 * (padded_f[0, 2:, 1:-1] - padded_f[0, :-2, 1:-1]) + 0.5 * (padded_f[1, 1:-1, 2:] - padded_f[1, 1:-1, :-2])
    flat_index = (elev_class[None] * LAND + correlation_cols).astype(jnp.int32)
    smb_ice = jnp.sum(correlation_weights * land_smb.reshape(-1)[flat_index], axis=0)
    surface = bed + thickness + time_step * (smb_ice - spread)
    numer = jnp.zeros((CLASSES * LAND,), jnp.float32).at[flat_index.reshape(-1)].add((correlation_weights * surface[None]).reshape(-1))
    denom = jnp.zeros((CLASSES * LAND,), jnp.float32).at[flat_index.reshape(-1)].add(correlation_weights.reshape(-1))
    land_surface = (numer / (denom + 1.0)).reshape(CLASSES, LAND)
    return velocity, surface, land_surface
```

```python
import functools
import jax
import jax.numpy as jnp
from jax import lax
from jax.experimental import pallas as pl
from jax.experimental.pallas import tpu as pltpu
from jax.sharding import PartitionSpec as P

KRYLOV = 4
MESH = pl.DeviceIdType.MESH
F32 = jnp.float32
BF = jnp.bfloat16
VM = pl.BlockSpec(memory_space=pltpu.VMEM)
SM = pl.BlockSpec(memory_space=pltpu.SMEM)
SLOTS = 128
HIGH = 64
NT = (((1,), (1,)), ((), ()))


def parts(x, count):
    out = []
    for _ in range(count):
        top = x.astype(BF)
        out.append(top)
        x = x - top.astype(F32)
    return out


def is_row(size, row):
    return lax.broadcasted_iota(jnp.int32, (size, row.shape[1]), 0) == row


def hot(size, row):
    return jnp.where(is_row(size, row), 1.0, 0.0).astype(BF)


def route_kernel(peers, turn_ref, cols_ref, class_ref, weights_ref, send_ref, cell_ref, most_ref, left_ref, right_ref, total_ref):
    width = cols_ref.shape[1]
    step = 8
    before = lax.broadcasted_iota(jnp.int32, (width, 2 * width), 0) < lax.broadcasted_iota(
        jnp.int32, (width, 2 * width), 1
    )
    ahead = jnp.where(before, 1.0, 0.0).astype(BF)
    first = turn_ref[0] * SLOTS
    most = jnp.zeros((peers, width), F32)
    for k in range(4):
        total_ref[...] = jnp.zeros_like(total_ref)

        def body(g, base):
            at = pl.multiple_of(k * 32 + g * step, step)
            cols = cols_ref[pl.ds(at, step), :]
            kind = class_ref[pl.ds(pl.multiple_of(g * step, step), step), :]
            dest = cols >> 9
            lane = lax.broadcasted_iota(jnp.int32, cols.shape, 1)
            row = lax.broadcasted_iota(jnp.int32, cols.shape, 0) + g * step
            whole = (kind * 4 + ((cols >> 7) & 3), cols & 127, row * 2 + (lane >> 7), lane & 127)
            fields = [v.astype(F32) for v in whole]
            w = weights_ref[pl.ds(at, step), :]
            w_top = w.astype(BF).astype(F32)
            fields += [w_top, w - w_top]
            for r in range(step):
                one = slice(r, r + 1)
                mask = is_row(peers, dest[one])
                picked = jnp.where(mask, 1.0, 0.0).astype(BF)
                counts = jnp.dot(picked, ahead, preferred_element_type=F32)
                rank = jnp.sum(jnp.where(mask, counts[:, :width] + base, 0.0), axis=0, keepdims=True)
                base = base + counts[:, width:]
                span = pl.ds(r * width, width)
                for f, value in enumerate(fields):
                    left_ref[f * peers : (f + 1) * peers, span] = picked * value[one].astype(BF)
                right_ref[:, span] = hot(SLOTS, rank.astype(jnp.int32) - first)
            total_ref[...] += lax.dot_general(left_ref[...], right_ref[...], NT, preferred_element_type=F32)
            return base

        base = lax.fori_loop(0, 32 // step, body, jnp.zeros((peers, width), F32))
        f = [total_ref[i * peers : (i + 1) * peers, :] for i in range(6)]
        send_ref[:, k, :] = f[0] * 128.0 + f[1]
        cell_ref[:, k, :] = f[2] * 128.0 + f[3]
        send_ref[:, 4 + k, :] = f[4] + f[5]
        most = jnp.maximum(most, base)
    most_ref[...] = jnp.broadcast_to(jnp.max(most, keepdims=True), most_ref.shape)


def route(turn, cols, kind, weights, peers=128):
    rows, width = 4 * cols.shape[1], cols.shape[2]
    return pl.pallas_call(
        functools.partial(route_kernel, peers),
        name="route",
        out_shape=(
            jax.ShapeDtypeStruct((peers, 8, SLOTS), F32),
            jax.ShapeDtypeStruct((peers, 4, SLOTS), F32),
            jax.ShapeDtypeStruct((8, 128), F32),
        ),
        in_specs=[SM, VM, VM, VM],
        out_specs=(VM, VM, VM),
        scratch_shapes=[
            pltpu.VMEM((6 * peers, 8 * width), BF),
            pltpu.VMEM((SLOTS, 8 * width), BF),
            pltpu.VMEM((6 * peers, SLOTS), F32),
        ],
        compiler_params=pltpu.CompilerParams(vmem_limit_bytes=48 << 20),
    )(turn, cols.reshape(rows, width), kind, weights.reshape(rows, width))


def spots(where):
    at = where.astype(jnp.int32)
    return at >> 7, at & 127


def table_terms(table):
    padded = jnp.concatenate([table, jnp.zeros((HIGH - table.shape[0], 128), F32)], axis=0) if table.shape[0] < HIGH else table
    return jnp.concatenate([p.astype(F32) for p in parts(padded, 3)], axis=0).T.astype(BF)


def look_up(terms, high, low_masks):
    stacked = jnp.concatenate([high] * 3, axis=0)
    found = jnp.dot(terms, stacked, preferred_element_type=F32)
    return jnp.sum(jnp.where(low_masks, found, 0.0), axis=0, keepdims=True)


def across(pieces):
    return jnp.concatenate(pieces, axis=1)


def add_in(total_ref, values, high, low):
    both = jnp.concatenate([high * v.astype(BF) for v in values], axis=0)
    total_ref[...] += lax.dot_general(both, low, NT, preferred_element_type=F32)


GROUP = 4


def flat_rows(tiles):
    return [tiles[s, k : k + 1, :] for s in range(tiles.shape[0]) for k in range(4)]


def owner_kernel(table_ref, got_ref, denom_ref, back_ref, terms_ref, total_ref):
    terms_ref[...] = table_terms(table_ref[...])
    total_ref[...] = jnp.zeros_like(total_ref)

    @pl.loop(0, got_ref.shape[0] // GROUP)
    def _(g):
        tile = got_ref[pl.ds(g * GROUP, GROUP), :, :]
        high, low = spots(tile[:, :4, :])
        w = across(flat_rows(tile[:, 4:, :]))
        high_hot = hot(HIGH, across(flat_rows(high)))
        low_mask = is_row(128, across(flat_rows(low)))
        low_hot = jnp.where(low_mask, 1.0, 0.0).astype(BF)
        w_top = w.astype(BF).astype(F32)
        add_in(total_ref, (w_top, w - w_top), high_hot, low_hot)
        found = look_up(terms_ref[...], high_hot, low_mask)
        for s in range(GROUP):
            for k in range(4):
                i = s * 4 + k
                back_ref[g * GROUP + s, k : k + 1, :] = found[:, i * 128 : (i + 1) * 128]

    denom_ref[...] = total_ref[:HIGH, :] + total_ref[HIGH:, :]


def owner(table, got):
    peers = got.shape[0]
    return pl.pallas_call(
        owner_kernel,
        name="owner",
        out_shape=(jax.ShapeDtypeStruct((HIGH, 128), F32), jax.ShapeDtypeStruct((peers, 4, SLOTS), F32)),
        in_specs=[VM, VM],
        out_specs=(VM, VM),
        scratch_shapes=[pltpu.VMEM((128, 3 * HIGH), BF), pltpu.VMEM((2 * HIGH, 128), F32)],
        compiler_params=pltpu.CompilerParams(vmem_limit_bytes=48 << 20),
    )(table, got)


def gather_kernel(table_ref, where_ref, out_ref, terms_ref):
    terms_ref[...] = table_terms(table_ref[...])

    @pl.loop(0, where_ref.shape[0] // GROUP)
    def _(g):
        high, low = spots(where_ref[pl.ds(g * GROUP, GROUP), :, :])
        found = look_up(
            terms_ref[...], hot(HIGH, across(flat_rows(high))), is_row(128, across(flat_rows(low)))
        )
        for s in range(GROUP):
            for k in range(4):
                i = s * 4 + k
                out_ref[g * GROUP + s, k : k + 1, :] = found[:, i * 128 : (i + 1) * 128]


def gather(table, where):
    return pl.pallas_call(
        gather_kernel,
        name="pick",
        out_shape=jax.ShapeDtypeStruct(where.shape, F32),
        in_specs=[VM, VM],
        out_specs=VM,
        scratch_shapes=[pltpu.VMEM((128, 3 * HIGH), BF)],
        compiler_params=pltpu.CompilerParams(vmem_limit_bytes=48 << 20),
    )(table, where)


def scatter_kernel(first, where_ref, weights_ref, values_ref, out_ref, total_ref):
    total_ref[...] = jnp.zeros_like(total_ref)

    @pl.loop(0, where_ref.shape[0] // GROUP)
    def _(g):
        span = pl.ds(g * GROUP, GROUP)
        high, low = spots(where_ref[span, :4, :])
        v = across(flat_rows(weights_ref[span, 4:, :] * values_ref[span, :, :]))
        v_top = v.astype(BF).astype(F32)
        add_in(
            total_ref,
            (v_top, v - v_top),
            hot(HIGH, across(flat_rows(high))),
            hot(128, across(flat_rows(low))),
        )

    out_ref[...] = total_ref[:HIGH, :] + total_ref[HIGH:, :]


def scatter(where, weights, values):
    return pl.pallas_call(
        functools.partial(scatter_kernel, 0),
        name="put",
        out_shape=jax.ShapeDtypeStruct((HIGH, 128), F32),
        in_specs=[VM, VM, VM],
        out_specs=VM,
        scratch_shapes=[pltpu.VMEM((2 * HIGH, 128), F32)],
        compiler_params=pltpu.CompilerParams(vmem_limit_bytes=48 << 20),
    )(where, weights, values)


def place():
    wide = lax.axis_size("tx")
    return lax.axis_index("ty") * wide + lax.axis_index("tx"), lax.axis_size("ty") * wide


def at(peer):
    wide = lax.axis_size("tx")
    return (peer // wide, peer % wide)


def meet(me, peers):
    barrier = pltpu.get_barrier_semaphore()

    @pl.loop(1, peers)
    def _(step):
        pl.semaphore_signal(barrier, inc=1, device_id=at((me + step) % peers), device_id_type=MESH)

    pl.semaphore_wait(barrier, peers - 1)


def exchange_kernel(send_ref, got_ref, out_sem, in_sem, own_sem):
    me, peers = place()
    own = pltpu.make_async_copy(send_ref.at[me], got_ref.at[me], own_sem)
    own.start()
    meet(me, peers)

    @pl.loop(1, peers)
    def _(step):
        peer = (me + step) % peers
        pltpu.make_async_remote_copy(
            send_ref.at[peer], got_ref.at[me], out_sem, in_sem, device_id=at(peer), device_id_type=MESH
        ).start()

    own.wait()
    others = pl.ds(0, peers - 1)
    whole = pltpu.make_async_remote_copy(
        send_ref.at[others], got_ref.at[others], out_sem, in_sem, device_id=at((me + 1) % peers), device_id_type=MESH
    )
    whole.wait()


def exchange(send, name, number):
    return pl.pallas_call(
        exchange_kernel,
        name=name,
        out_shape=jax.ShapeDtypeStruct(send.shape, send.dtype),
        in_specs=[VM],
        out_specs=VM,
        scratch_shapes=[pltpu.SemaphoreType.DMA] * 3,
        compiler_params=pltpu.CompilerParams(collective_id=number, has_side_effects=True),
    )(send)


def total_kernel(part_ref, sum_ref, got_ref, out_sem, in_sem):
    me, peers = place()
    meet(me, peers)

    @pl.loop(1, peers)
    def _(step):
        peer = (me + step) % peers
        pltpu.make_async_remote_copy(
            part_ref, got_ref.at[me], out_sem, in_sem, device_id=at(peer), device_id_type=MESH
        ).start()

    got_ref[pl.ds(me, 1)] = part_ref[...][None]
    others = pl.ds(0, peers - 1)
    whole = pltpu.make_async_remote_copy(
        got_ref.at[others], got_ref.at[others], out_sem, in_sem, device_id=at((me + 1) % peers), device_id_type=MESH
    )
    whole.wait()
    everyone = got_ref[...]
    row = lax.broadcasted_iota(jnp.int32, sum_ref.shape, 0)
    sum_ref[...] = jnp.where(row < 7, jnp.sum(everyone, axis=0), jnp.max(everyone, axis=0))


def total(part, name, number, peers=128):
    return pl.pallas_call(
        total_kernel,
        name=name,
        out_shape=jax.ShapeDtypeStruct(part.shape, part.dtype),
        in_specs=[VM],
        out_specs=VM,
        scratch_shapes=[pltpu.VMEM((peers, *part.shape), part.dtype)] + [pltpu.SemaphoreType.DMA] * 2,
        compiler_params=pltpu.CompilerParams(collective_id=number, has_side_effects=True),
    )(part)


eps_strain = 0.1
vert_coupling = 2.0
time_step = 0.5


def padded_2(array, sides, width):
    edges = {}
    for axis, dim in sides:
        devices, length = (lax.axis_size(axis), array.shape[dim])
        up = [(i, (i + 1) % devices) for i in range(devices - 1)]
        last = lax.slice_in_dim(array, length - width, length, axis=dim)
        initial = lax.slice_in_dim(array, 0, width, axis=dim)
        edges[dim] = (
            lax.ppermute(last, axis, up),
            lax.ppermute(initial, axis, [(b, a) for a, b in up]),
        )
    done = []
    for _, dim in sides:
        low, high = edges[dim]
        around = [(width, width) if d in done else (0, 0) for d in range(array.ndim)]
        array = jnp.concatenate([jnp.pad(low, around), array, jnp.pad(high, around)], axis=dim)
        done.append(dim)
    return array


def strain_viscosity(padded, stiffness):
    flow_x = padded[0]
    flow_y = padded[1]
    grad_xx = 0.5 * (flow_x[:, 2:, 1:-1] - flow_x[:, :-2, 1:-1])
    grad_yy = 0.5 * (flow_y[:, 1:-1, 2:] - flow_y[:, 1:-1, :-2])
    grad_xy = 0.5 * (flow_x[:, 1:-1, 2:] - flow_x[:, 1:-1, :-2])
    grad_yx = 0.5 * (flow_y[:, 2:, 1:-1] - flow_y[:, :-2, 1:-1])
    inner_x = flow_x[:, 1:-1, 1:-1]
    inner_y = flow_y[:, 1:-1, 1:-1]
    shear_x = jnp.concatenate([inner_x[1:] - inner_x[:-1], jnp.zeros_like(inner_x[:1])], axis=0)
    shear_y = jnp.concatenate([inner_y[1:] - inner_y[:-1], jnp.zeros_like(inner_y[:1])], axis=0)
    rate = grad_xx * grad_xx + grad_yy * grad_yy + grad_xx * grad_yy
    rate = rate + 0.25 * (grad_xy + grad_yx) ** 2 + 0.25 * (shear_x * shear_x + shear_y * shear_y)
    return stiffness * (eps_strain + rate) ** (-1.0 / 3.0)


def face_weights(padded_mu):
    center = padded_mu[:, 1:-1, 1:-1]
    x_plus = 0.5 * (center + padded_mu[:, 2:, 1:-1])
    x_minus = 0.5 * (center + padded_mu[:, :-2, 1:-1])
    y_plus = 0.5 * (center + padded_mu[:, 1:-1, 2:])
    y_minus = 0.5 * (center + padded_mu[:, 1:-1, :-2])
    z_face = 0.5 * (center[1:] + center[:-1])
    zeros_layer = jnp.zeros_like(center[:1])
    z_plus = jnp.concatenate([z_face, zeros_layer], axis=0)
    z_minus = jnp.concatenate([zeros_layer, z_face], axis=0)
    return (x_plus, x_minus, y_plus, y_minus, z_plus, z_minus)


def stokes_apply(padded, faces, beta):
    x_plus, x_minus, y_plus, y_minus, z_plus, z_minus = faces
    center = padded[:, :, 1:-1, 1:-1]
    lateral_x = jnp.array([4.0, 1.0], dtype=jnp.float32).reshape(2, 1, 1, 1)
    lateral_y = jnp.array([1.0, 4.0], dtype=jnp.float32).reshape(2, 1, 1, 1)
    term_x = lateral_x * (
        x_plus * (center - padded[:, :, 2:, 1:-1]) + x_minus * (center - padded[:, :, :-2, 1:-1])
    )
    term_y = lateral_y * (
        y_plus * (center - padded[:, :, 1:-1, 2:]) + y_minus * (center - padded[:, :, 1:-1, :-2])
    )
    zeros_level = jnp.zeros_like(center[:, :1])
    above = jnp.concatenate([center[:, 1:], zeros_level], axis=1)
    below = jnp.concatenate([zeros_level, center[:, :-1]], axis=1)
    term_z = vert_coupling * (z_plus * (center - above) + z_minus * (center - below))
    bottom = (jnp.arange(center.shape[1]) == 0).astype(jnp.float32).reshape(1, -1, 1, 1)
    return term_x + term_y + term_z + bottom * beta * center


def masked_apply(field, faces, beta, mask):
    padded = padded_2(mask * field, (("ty", 2), ("tx", 3)), 1)
    return mask * stokes_apply(padded, faces, beta) + (1.0 - mask) * field


def summed(residual, image, most):
    ones = jnp.ones((1, 128), jnp.float32)
    own = jnp.concatenate(
        [jnp.sum(residual * residual) * ones, jnp.sum(residual * image) * ones]
        + [0.0 * ones] * 5
        + [most[:1]],
        axis=0,
    )
    everyone = total(own, "total", 1)
    return everyone[0, 0], everyone[1, 0], everyone[7, 0]


def krylov_solve(solution, rhs, faces, beta, mask, most):
    residual = rhs - masked_apply(solution, faces, beta, mask)
    image = masked_apply(residual, faces, beta, mask)
    norm_now, product, most_of_all = summed(residual, image, most)
    step_size = norm_now / product

    def merged_step(index, carry):
        solution, residual, direction, along, norm_now, step_size = carry
        solution = solution + step_size * direction
        residual = residual - step_size * along
        image = masked_apply(residual, faces, beta, mask)
        norm_next, product, _ = summed(residual, image, most)
        ratio = norm_next / norm_now
        step_next = norm_next / (product - ratio * norm_next / step_size)
        direction = residual + ratio * direction
        along = image + ratio * along
        return (solution, residual, direction, along, norm_next, step_next)

    carry = lax.fori_loop(
        0, KRYLOV - 1, merged_step, (solution, residual, residual, image, norm_now, step_size)
    )
    return carry[0] + carry[5] * carry[2], most_of_all


def on_device(
    velocity_start,
    stiffness,
    beta,
    ice_mask,
    thickness,
    bed,
    land_smb,
    elev_class,
    correlation_cols,
    correlation_weights,
):
    mask = ice_mask.astype(jnp.float32)
    levels = velocity_start.shape[1]
    rows = velocity_start.shape[2]
    cols = velocity_start.shape[3]
    own_table = land_smb.reshape(-1, 128)

    def turn(number):
        return route(
            jnp.full((1,), number, jnp.int32), correlation_cols, elev_class, correlation_weights
        )

    def balance_and_weights(send, cell, got, swap):
        denom, found = owner(own_table, got)
        return scatter(cell, send, swap(found)), denom

    def plain_swap(array):
        return lax.all_to_all(array, ("ty", "tx"), 0, 0, tiled=True)

    send, cell, most = turn(0)
    got = exchange(send, "to_owner", 2)
    smb_ice, denom = balance_and_weights(send, cell, got, lambda a: exchange(a, "from_owner", 3))

    surface_old = bed + thickness
    combined = jnp.concatenate(
        [velocity_start.reshape(2 * levels, rows, cols), surface_old[None]], axis=0
    )
    padded_all = padded_2(combined, (("ty", 1), ("tx", 2)), 1)
    padded_s = padded_all[-1]
    slope_x = 0.5 * (padded_s[2:, 1:-1] - padded_s[:-2, 1:-1])
    slope_y = 0.5 * (padded_s[1:-1, 2:] - padded_s[1:-1, :-2])
    drive = -(mask * thickness) * jnp.stack([slope_x, slope_y])
    rhs = drive[:, None] * jnp.ones((1, levels, 1, 1), jnp.float32)
    padded_vel = padded_all[:-1].reshape(2, levels, rows + 2, cols + 2)
    visc = strain_viscosity(padded_vel, stiffness)
    padded_mu = padded_2(visc, (("ty", 1), ("tx", 2)), 1)
    faces = face_weights(padded_mu)
    velocity, most = krylov_solve(velocity_start, rhs, faces, beta, mask, most)
    turns = ((most.astype(jnp.int32) + SLOTS - 1) // SLOTS).astype(jnp.int32)

    def more_balance(carry):
        number, smb, weights = carry
        send, cell, _ = turn(number)
        add_smb, add_weights = balance_and_weights(send, cell, plain_swap(send), plain_swap)
        return number + 1, smb + add_smb, weights + add_weights

    def unfinished(carry):
        return carry[0] < turns

    _, smb_ice, denom = lax.while_loop(unfinished, more_balance, (jnp.int32(1), smb_ice, denom))
    smb_ice = smb_ice.reshape(rows, cols)
    mean_flow = jnp.mean(velocity, axis=1)
    padded_f = padded_2(thickness * mean_flow, (("ty", 1), ("tx", 2)), 1)
    spread = 0.5 * (padded_f[0, 2:, 1:-1] - padded_f[0, :-2, 1:-1]) + 0.5 * (
        padded_f[1, 1:-1, 2:] - padded_f[1, 1:-1, :-2]
    )
    surface = bed + thickness + time_step * (smb_ice - spread)
    surface_rows = surface.reshape(-1, 128)
    numer = scatter(got, got, exchange(gather(surface_rows, cell), "to_land", 4))

    def more_numer(carry):
        number, numer = carry
        send, cell, _ = turn(number)
        got = plain_swap(send)
        return number + 1, numer + scatter(got, got, plain_swap(gather(surface_rows, cell)))

    _, numer = lax.while_loop(unfinished, more_numer, (jnp.int32(1), numer))
    used = own_table.shape[0]
    land_surface = (numer[:used] / (denom[:used] + 1.0)).reshape(land_smb.shape)
    return (velocity, surface, land_surface)


def solution(mesh):
    every = ("ty", "tx")
    return jax.shard_map(
        on_device,
        mesh=mesh,
        in_specs=(
            P(None, None, "ty", "tx"),
            P(None, "ty", "tx"),
            P("ty", "tx"),
            P("ty", "tx"),
            P("ty", "tx"),
            P("ty", "tx"),
            P(None, every),
            P("ty", "tx"),
            P(None, "ty", "tx"),
            P(None, "ty", "tx"),
        ),
        out_specs=(P(None, None, "ty", "tx"), P("ty", "tx"), P(None, every)),
        check_vma=False,
    )
```

```python
import functools
import jax
import jax.numpy as jnp
from jax import lax
from jax.experimental import pallas as pl
from jax.experimental.pallas import tpu as pltpu
from jax.sharding import PartitionSpec as P

MESH = pl.DeviceIdType.MESH
F32 = jnp.float32
BF = jnp.bfloat16
VM = pl.BlockSpec(memory_space=pltpu.VMEM)
SM = pl.BlockSpec(memory_space=pltpu.SMEM)
SLOTS = 128
HIGH = 64
NT = (((1,), (1,)), ((), ()))


def parts(x, count):
    out = []
    for _ in range(count):
        top = x.astype(BF)
        out.append(top)
        x = x - top.astype(F32)
    return out


def is_row(size, row):
    return lax.broadcasted_iota(jnp.int32, (size, row.shape[1]), 0) == row


def hot(size, row):
    return jnp.where(is_row(size, row), 1.0, 0.0).astype(BF)


def route_kernel(peers, turn_ref, cols_ref, class_ref, weights_ref, send_ref, cell_ref, most_ref, left_ref, right_ref, total_ref):
    width = cols_ref.shape[1]
    step = 8
    before = lax.broadcasted_iota(jnp.int32, (width, 2 * width), 0) < lax.broadcasted_iota(
        jnp.int32, (width, 2 * width), 1
    )
    ahead = jnp.where(before, 1.0, 0.0).astype(BF)
    first = turn_ref[0] * SLOTS
    most = jnp.zeros((peers, width), F32)
    for k in range(4):
        total_ref[...] = jnp.zeros_like(total_ref)

        def body(g, base):
            at = pl.multiple_of(k * 32 + g * step, step)
            cols = cols_ref[pl.ds(at, step), :]
            kind = class_ref[pl.ds(pl.multiple_of(g * step, step), step), :]
            dest = cols >> 9
            lane = lax.broadcasted_iota(jnp.int32, cols.shape, 1)
            row = lax.broadcasted_iota(jnp.int32, cols.shape, 0) + g * step
            whole = (kind * 4 + ((cols >> 7) & 3), cols & 127, row * 2 + (lane >> 7), lane & 127)
            fields = [v.astype(F32) for v in whole]
            w = weights_ref[pl.ds(at, step), :]
            w_top = w.astype(BF).astype(F32)
            fields += [w_top, w - w_top]
            for r in range(step):
                one = slice(r, r + 1)
                mask = is_row(peers, dest[one])
                picked = jnp.where(mask, 1.0, 0.0).astype(BF)
                counts = jnp.dot(picked, ahead, preferred_element_type=F32)
                rank = jnp.sum(jnp.where(mask, counts[:, :width] + base, 0.0), axis=0, keepdims=True)
                base = base + counts[:, width:]
                span = pl.ds(r * width, width)
                for f, value in enumerate(fields):
                    left_ref[f * peers : (f + 1) * peers, span] = picked * value[one].astype(BF)
                right_ref[:, span] = hot(SLOTS, rank.astype(jnp.int32) - first)
            total_ref[...] += lax.dot_general(left_ref[...], right_ref[...], NT, preferred_element_type=F32)
            return base

        base = lax.fori_loop(0, 32 // step, body, jnp.zeros((peers, width), F32))
        f = [total_ref[i * peers : (i + 1) * peers, :] for i in range(6)]
        send_ref[:, k, :] = f[0] * 128.0 + f[1]
        cell_ref[:, k, :] = f[2] * 128.0 + f[3]
        send_ref[:, 4 + k, :] = f[4] + f[5]
        most = jnp.maximum(most, base)
    most_ref[...] = jnp.broadcast_to(jnp.max(most, keepdims=True), most_ref.shape)


def route(turn, cols, kind, weights, peers=128):
    rows, width = 4 * cols.shape[1], cols.shape[2]
    return pl.pallas_call(
        functools.partial(route_kernel, peers),
        name="route",
        out_shape=(
            jax.ShapeDtypeStruct((peers, 8, SLOTS), F32),
            jax.ShapeDtypeStruct((peers, 4, SLOTS), F32),
            jax.ShapeDtypeStruct((8, 128), F32),
        ),
        in_specs=[SM, VM, VM, VM],
        out_specs=(VM, VM, VM),
        scratch_shapes=[
            pltpu.VMEM((6 * peers, 8 * width), BF),
            pltpu.VMEM((SLOTS, 8 * width), BF),
            pltpu.VMEM((6 * peers, SLOTS), F32),
        ],
        compiler_params=pltpu.CompilerParams(vmem_limit_bytes=48 << 20),
    )(turn, cols.reshape(rows, width), kind, weights.reshape(rows, width))


def spots(where):
    at = where.astype(jnp.int32)
    return at >> 7, at & 127


def table_terms(table):
    padded = jnp.concatenate([table, jnp.zeros((HIGH - table.shape[0], 128), F32)], axis=0) if table.shape[0] < HIGH else table
    return jnp.concatenate([p.astype(F32) for p in parts(padded, 3)], axis=0).T.astype(BF)


def look_up(terms, high, low_masks):
    stacked = jnp.concatenate([high] * 3, axis=0)
    found = jnp.dot(terms, stacked, preferred_element_type=F32)
    return jnp.sum(jnp.where(low_masks, found, 0.0), axis=0, keepdims=True)


def across(pieces):
    return jnp.concatenate(pieces, axis=1)


def add_in(total_ref, values, high, low):
    both = jnp.concatenate([high * v.astype(BF) for v in values], axis=0)
    total_ref[...] += lax.dot_general(both, low, NT, preferred_element_type=F32)


GROUP = 4


def flat_rows(tiles):
    return [tiles[s, k : k + 1, :] for s in range(tiles.shape[0]) for k in range(4)]


def owner_kernel(table_ref, got_ref, denom_ref, back_ref, terms_ref, total_ref):
    terms_ref[...] = table_terms(table_ref[...])
    total_ref[...] = jnp.zeros_like(total_ref)

    @pl.loop(0, got_ref.shape[0] // GROUP)
    def _(g):
        tile = got_ref[pl.ds(g * GROUP, GROUP), :, :]
        high, low = spots(tile[:, :4, :])
        w = across(flat_rows(tile[:, 4:, :]))
        high_hot = hot(HIGH, across(flat_rows(high)))
        low_mask = is_row(128, across(flat_rows(low)))
        low_hot = jnp.where(low_mask, 1.0, 0.0).astype(BF)
        w_top = w.astype(BF).astype(F32)
        add_in(total_ref, (w_top, w - w_top), high_hot, low_hot)
        found = look_up(terms_ref[...], high_hot, low_mask)
        for s in range(GROUP):
            for k in range(4):
                i = s * 4 + k
                back_ref[g * GROUP + s, k : k + 1, :] = found[:, i * 128 : (i + 1) * 128]

    denom_ref[...] = total_ref[:HIGH, :] + total_ref[HIGH:, :]


def owner(table, got):
    peers = got.shape[0]
    return pl.pallas_call(
        owner_kernel,
        name="owner",
        out_shape=(jax.ShapeDtypeStruct((HIGH, 128), F32), jax.ShapeDtypeStruct((peers, 4, SLOTS), F32)),
        in_specs=[VM, VM],
        out_specs=(VM, VM),
        scratch_shapes=[pltpu.VMEM((128, 3 * HIGH), BF), pltpu.VMEM((2 * HIGH, 128), F32)],
        compiler_params=pltpu.CompilerParams(vmem_limit_bytes=48 << 20),
    )(table, got)


def gather_kernel(table_ref, where_ref, out_ref, terms_ref):
    terms_ref[...] = table_terms(table_ref[...])

    @pl.loop(0, where_ref.shape[0] // GROUP)
    def _(g):
        high, low = spots(where_ref[pl.ds(g * GROUP, GROUP), :, :])
        found = look_up(
            terms_ref[...], hot(HIGH, across(flat_rows(high))), is_row(128, across(flat_rows(low)))
        )
        for s in range(GROUP):
            for k in range(4):
                i = s * 4 + k
                out_ref[g * GROUP + s, k : k + 1, :] = found[:, i * 128 : (i + 1) * 128]


def gather(table, where):
    return pl.pallas_call(
        gather_kernel,
        name="pick",
        out_shape=jax.ShapeDtypeStruct(where.shape, F32),
        in_specs=[VM, VM],
        out_specs=VM,
        scratch_shapes=[pltpu.VMEM((128, 3 * HIGH), BF)],
        compiler_params=pltpu.CompilerParams(vmem_limit_bytes=48 << 20),
    )(table, where)


def scatter_kernel(first, where_ref, weights_ref, values_ref, out_ref, total_ref):
    total_ref[...] = jnp.zeros_like(total_ref)

    @pl.loop(0, where_ref.shape[0] // GROUP)
    def _(g):
        span = pl.ds(g * GROUP, GROUP)
        high, low = spots(where_ref[span, :4, :])
        v = across(flat_rows(weights_ref[span, 4:, :] * values_ref[span, :, :]))
        v_top = v.astype(BF).astype(F32)
        add_in(
            total_ref,
            (v_top, v - v_top),
            hot(HIGH, across(flat_rows(high))),
            hot(128, across(flat_rows(low))),
        )

    out_ref[...] = total_ref[:HIGH, :] + total_ref[HIGH:, :]


def scatter(where, weights, values):
    return pl.pallas_call(
        functools.partial(scatter_kernel, 0),
        name="put",
        out_shape=jax.ShapeDtypeStruct((HIGH, 128), F32),
        in_specs=[VM, VM, VM],
        out_specs=VM,
        scratch_shapes=[pltpu.VMEM((2 * HIGH, 128), F32)],
        compiler_params=pltpu.CompilerParams(vmem_limit_bytes=48 << 20),
    )(where, weights, values)


def place():
    wide = lax.axis_size("tx")
    return lax.axis_index("ty") * wide + lax.axis_index("tx"), lax.axis_size("ty") * wide


def at(peer):
    wide = lax.axis_size("tx")
    return (peer // wide, peer % wide)


def meet(me, peers):
    barrier = pltpu.get_barrier_semaphore()

    @pl.loop(1, peers)
    def _(step):
        pl.semaphore_signal(barrier, inc=1, device_id=at((me + step) % peers), device_id_type=MESH)

    pl.semaphore_wait(barrier, peers - 1)


def exchange_kernel(send_ref, got_ref, out_sem, in_sem, own_sem):
    me, peers = place()
    own = pltpu.make_async_copy(send_ref.at[me], got_ref.at[me], own_sem)
    own.start()
    meet(me, peers)

    @pl.loop(1, peers)
    def _(step):
        peer = (me + step) % peers
        pltpu.make_async_remote_copy(
            send_ref.at[peer], got_ref.at[me], out_sem, in_sem, device_id=at(peer), device_id_type=MESH
        ).start()

    own.wait()
    others = pl.ds(0, peers - 1)
    whole = pltpu.make_async_remote_copy(
        send_ref.at[others], got_ref.at[others], out_sem, in_sem, device_id=at((me + 1) % peers), device_id_type=MESH
    )
    whole.wait()


def exchange(send, name, number):
    return pl.pallas_call(
        exchange_kernel,
        name=name,
        out_shape=jax.ShapeDtypeStruct(send.shape, send.dtype),
        in_specs=[VM],
        out_specs=VM,
        scratch_shapes=[pltpu.SemaphoreType.DMA] * 3,
        compiler_params=pltpu.CompilerParams(collective_id=number, has_side_effects=True),
    )(send)


def joined(tiles):
    row = lax.broadcasted_iota(jnp.int32, tiles.shape[1:], 0)
    return jnp.where(row < 7, jnp.sum(tiles, axis=0), jnp.max(tiles, axis=0))


def total_kernel(part_ref, sum_ref, near_ref, half_ref, far_ref, near_out, near_in, far_out, far_in):
    y, x = lax.axis_index("ty"), lax.axis_index("tx")
    tall, wide = lax.axis_size("ty"), lax.axis_size("tx")
    core, chip = x % 2, x // 2
    near, far = tall * 2, wide // 2
    me = y * 2 + core
    near_ids = [(me + i) % near for i in range(1, near)]
    near_devices = [(i // 2, chip * 2 + i % 2) for i in near_ids]
    far_devices = [(y, ((chip + i) % far) * 2 + core) for i in range(1, far)]
    barrier = pltpu.get_barrier_semaphore()
    for device in near_devices + far_devices:
        pl.semaphore_signal(barrier, inc=1, device_id=device, device_id_type=MESH)
    pl.semaphore_wait(barrier, near + far - 2)
    for device in near_devices:
        pltpu.make_async_remote_copy(
            part_ref, near_ref.at[me], near_out, near_in, device_id=device, device_id_type=MESH
        ).start()
    near_ref[pl.ds(me, 1)] = part_ref[...][None]
    whole = pl.ds(0, near - 1)
    pltpu.make_async_remote_copy(
        near_ref.at[whole], near_ref.at[whole], near_out, near_in, device_id=near_devices[0], device_id_type=MESH
    ).wait()
    half = joined(near_ref[...])
    half_ref[...] = half
    for device in far_devices:
        pltpu.make_async_remote_copy(
            half_ref, far_ref.at[chip], far_out, far_in, device_id=device, device_id_type=MESH
        ).start()
    far_ref[pl.ds(chip, 1)] = half[None]
    whole = pl.ds(0, far - 1)
    pltpu.make_async_remote_copy(
        far_ref.at[whole], far_ref.at[whole], far_out, far_in, device_id=far_devices[0], device_id_type=MESH
    ).wait()
    sum_ref[...] = joined(far_ref[...])


def total(part, name, number):
    tall, wide = lax.axis_size("ty"), lax.axis_size("tx")
    shape = part.shape
    return pl.pallas_call(
        total_kernel,
        name=name,
        out_shape=jax.ShapeDtypeStruct(shape, part.dtype),
        in_specs=[VM],
        out_specs=VM,
        scratch_shapes=[
            pltpu.VMEM((tall * 2, *shape), part.dtype),
            pltpu.VMEM(shape, part.dtype),
            pltpu.VMEM((wide // 2, *shape), part.dtype),
        ]
        + [pltpu.SemaphoreType.DMA] * 4,
        compiler_params=pltpu.CompilerParams(collective_id=number, has_side_effects=True),
    )(part)


LEV = 10
ROWS, COLS = 32, 256
TALL, LONG = 48, 384
RIM = 8
PLANES = 3 * LEV + 4
MASK, THICK, BED, BETA = range(3 * LEV, PLANES)
PACKS = 3
ALL_ROWS = pl.ds(0, ROWS)


def halo_kernel(vel_ref, stiff_ref, mask_ref, thick_ref, bed_ref, beta_ref, out_ref, left_ref, right_ref, from_right, from_left, out_sem, in_sem):
    y, x = lax.axis_index("ty"), lax.axis_index("tx")
    tall, wide = lax.axis_size("ty"), lax.axis_size("tx")
    lane = lax.broadcasted_iota(jnp.int32, (ROWS, 128), 1)
    left = [jnp.zeros((ROWS, 128), F32)] * PACKS
    right = [jnp.zeros((ROWS, 128), F32)] * PACKS
    for p in range(PLANES):
        if p < 2 * LEV:
            plane = vel_ref[p]
        elif p < 3 * LEV:
            plane = stiff_ref[p - 2 * LEV]
        elif p == MASK:
            plane = mask_ref[...].astype(F32)
        else:
            plane = {THICK: thick_ref, BED: bed_ref, BETA: beta_ref}[p][...]
        out_ref[p, :ROWS, :COLS] = plane
        pack, k = p // 16, p % 16
        here = (lane >= RIM * k) & (lane < RIM * (k + 1))
        first, last = plane[:, :128], plane[:, COLS - 128 :]
        left[pack] = jnp.where(here, pltpu.roll(first, RIM * k, 1) if k else first, left[pack])
        turn = (RIM * k + RIM) % 128
        right[pack] = jnp.where(here, pltpu.roll(last, turn, 1) if turn else last, right[pack])
    for i in range(PACKS):
        left_ref[i] = left[i]
        right_ref[i] = right[i]
    around = [(a, b) for a in (-1, 0, 1) for b in (-1, 0, 1) if (a, b) != (0, 0)]
    where = [((y + a + tall) % tall, (x + b + wide) % wide) for a, b in around]
    barrier = pltpu.get_barrier_semaphore()
    for device in where:
        pl.semaphore_signal(barrier, inc=1, device_id=device, device_id_type=MESH)
    pl.semaphore_wait(barrier, len(where))
    copies = []
    for i, ((a, b), device) in enumerate(zip(around, where)):
        rows = {-1: pl.ds(0, RIM), 0: ALL_ROWS, 1: pl.ds(ROWS - RIM, RIM)}[a]
        there = {-1: pl.ds(ROWS, RIM), 0: ALL_ROWS, 1: pl.ds(TALL - RIM, RIM)}[a]
        if b == 0:
            ends = out_ref.at[:, rows, pl.ds(0, COLS)], out_ref.at[:, there, pl.ds(0, COLS)]
        elif b < 0:
            ends = left_ref.at[:, rows, :], from_right.at[:, there, :]
        else:
            ends = right_ref.at[:, rows, :], from_left.at[:, there, :]
        copies.append(
            pltpu.make_async_remote_copy(
                *ends, out_sem.at[i], in_sem.at[i], device_id=device, device_id_type=MESH
            )
        )
        copies[-1].start()
    for copy in copies:
        copy.wait()
    row = lax.broadcasted_iota(jnp.int32, (TALL, 128), 0)
    lane = lax.broadcasted_iota(jnp.int32, (TALL, 128), 1)
    inside = (row < ROWS) | ((row < ROWS + RIM) & (y < tall - 1)) | ((row >= TALL - RIM) & (y > 0))
    on_right = inside & (lane < RIM) & (x < wide - 1)
    on_left = inside & (lane >= 128 - RIM) & (x > 0)
    rights = [from_right[i] for i in range(PACKS)]
    lefts = [from_left[i] for i in range(PACKS)]
    for p in range(PLANES):
        pack, k = p // 16, p % 16
        to_right = pltpu.roll(rights[pack], 128 - RIM * k, 1) if k else rights[pack]
        turn = (128 - RIM - RIM * k) % 128
        to_left = pltpu.roll(lefts[pack], turn, 1) if turn else lefts[pack]
        out_ref[p, :, COLS:] = jnp.where(on_right, to_right, jnp.where(on_left, to_left, 0.0))

    @pl.when(y == tall - 1)
    def _():
        out_ref[:, ROWS : ROWS + RIM, :COLS] = jnp.zeros((PLANES, RIM, COLS), F32)

    @pl.when(y == 0)
    def _():
        out_ref[:, TALL - RIM :, :COLS] = jnp.zeros((PLANES, RIM, COLS), F32)


def with_halo(velocity, stiffness, mask, thickness, bed, beta):
    return pl.pallas_call(
        halo_kernel,
        name="halo",
        out_shape=jax.ShapeDtypeStruct((PLANES, TALL, LONG), F32),
        in_specs=[VM] * 6,
        out_specs=VM,
        scratch_shapes=[
            pltpu.VMEM((PACKS, ROWS, 128), F32),
            pltpu.VMEM((PACKS, ROWS, 128), F32),
            pltpu.VMEM((PACKS, TALL, 128), F32),
            pltpu.VMEM((PACKS, TALL, 128), F32),
            pltpu.SemaphoreType.DMA((8,)),
            pltpu.SemaphoreType.DMA((8,)),
        ],
        compiler_params=pltpu.CompilerParams(collective_id=5, has_side_effects=True),
    )(velocity.reshape(2 * LEV, ROWS, COLS), stiffness, mask, thickness, bed, beta)


def next_row(a):
    return pltpu.roll(a, a.shape[0] - 1, 0)


def last_row(a):
    return pltpu.roll(a, 1, 0)


def next_col(a):
    return pltpu.roll(a, a.shape[1] - 1, 1)


def last_col(a):
    return pltpu.roll(a, 1, 1)


def folded(a, b):
    inner = a[:ROWS, :COLS] * b[:ROWS, :COLS]
    return inner[0:8] + inner[8:16] + inner[16:24] + inner[24:32]


def apply_level(source, level, gx_ref, gy_ref, gz_ref, mask, friction):
    gx, gy = gx_ref[level], gy_ref[level]
    over, under = gz_ref[level + 1], gz_ref[level]
    upper = jnp.minimum(level + 1, LEV - 1)
    lower = jnp.maximum(level - 1, 0)
    results = []
    for c, (along_x, along_y) in enumerate(((2.0, 0.5), (0.5, 2.0))):
        w = source(c, level)
        held = mask * w
        flow_x = gx * (held - next_row(held))
        flow_y = gy * (held - next_col(held))
        value = along_x * (flow_x - last_row(flow_x)) + along_y * (flow_y - last_col(flow_y))
        value = value + over * (held - mask * source(c, upper)) + under * (held - mask * source(c, lower))
        value = value + friction * held
        results.append(jnp.where(mask > 0.0, value, w))
    return results


def planes_of(ref):
    return lambda c, level: ref[c * LEV + level]


def tile_of(pairs, last=None):
    lane = lax.broadcasted_iota(jnp.int32, (1, 128), 1)
    rows = [jnp.where(lane < 64, a, b) for a, b in pairs]
    rows += [jnp.zeros((1, 128), F32)] * (7 - len(rows))
    rows.append(jnp.zeros((1, 128), F32) if last is None else last)
    return jnp.concatenate(rows, axis=0)


def summed(sums_ref, count):
    return [jnp.sum(sums_ref[i], keepdims=True) for i in range(count)]


def begin_kernel(all_ref, most_ref, r0_ref, v1_ref, v2_ref, gx_ref, gy_ref, gz_ref, part_ref, mu_ref, sums_ref):
    sums_ref[...] = jnp.zeros_like(sums_ref)
    mask = all_ref[MASK]
    beta = all_ref[BETA]

    @pl.loop(0, LEV)
    def _(level):
        upper = jnp.minimum(level + 1, LEV - 1)
        u, v = all_ref[level], all_ref[LEV + level]
        grad_xx = 0.5 * (next_row(u) - last_row(u))
        grad_yy = 0.5 * (next_col(v) - last_col(v))
        cross = 0.5 * (next_col(u) - last_col(u)) + 0.5 * (next_row(v) - last_row(v))
        shear_x = all_ref[upper] - u
        shear_y = all_ref[LEV + upper] - v
        rate = grad_xx * grad_xx + grad_yy * grad_yy + grad_xx * grad_yy
        rate = rate + 0.25 * (cross * cross) + 0.25 * (shear_x * shear_x + shear_y * shear_y)
        base = rate + 0.1
        root = jnp.exp(jnp.log(base) * (-1.0 / 3.0))
        root = root * (4.0 - base * (root * root * root)) * (1.0 / 3.0)
        mu_ref[level] = all_ref[2 * LEV + level] * root

    gz_ref[0] = jnp.zeros((TALL, LONG), F32)
    gz_ref[LEV] = jnp.zeros((TALL, LONG), F32)

    @pl.loop(0, LEV)
    def _(level):
        mu = mu_ref[level]
        gx_ref[level] = mu + next_row(mu)
        gy_ref[level] = mu + next_col(mu)

    @pl.loop(1, LEV)
    def _(level):
        gz_ref[level] = mu_ref[level - 1] + mu_ref[level]

    s0 = all_ref[BED] + all_ref[THICK]
    force = -(mask * all_ref[THICK])
    drive = (force * (0.5 * (next_row(s0) - last_row(s0))), force * (0.5 * (next_col(s0) - last_col(s0))))

    def at_level(level):
        return jnp.where(level == 0, beta, 0.0)

    @pl.loop(0, LEV)
    def _(level):
        for c, value in enumerate(apply_level(planes_of(all_ref), level, gx_ref, gy_ref, gz_ref, mask, at_level(level))):
            r = drive[c] - value
            r0_ref[c * LEV + level] = r
            sums_ref[0] += folded(r, r)

    @pl.loop(0, LEV)
    def _(level):
        for c, value in enumerate(apply_level(planes_of(r0_ref), level, gx_ref, gy_ref, gz_ref, mask, at_level(level))):
            v1_ref[c * LEV + level] = value
            sums_ref[1] += folded(value, r0_ref[c * LEV + level])
            sums_ref[2] += folded(value, value)

    @pl.loop(0, LEV)
    def _(level):
        for c, value in enumerate(apply_level(planes_of(v1_ref), level, gx_ref, gy_ref, gz_ref, mask, at_level(level))):
            v2_ref[c * LEV + level] = value
            sums_ref[3] += folded(value, v1_ref[c * LEV + level])

    part_ref[...] = tile_of([(s, s) for s in summed(sums_ref, 4)], most_ref[:1, :])


def first_scalars(total_ref):
    m0, m1, m2, m3 = (total_ref[i : i + 1, 0:1] for i in range(4))
    a0 = m0 / m1
    rr1 = a0 * a0 * m2 - m0
    b1 = rr1 / m0
    c = 1.0 + b1
    along = c * c * m1 - 2.0 * c * a0 * m2 + a0 * a0 * m3
    a1 = rr1 / along
    return a0, a1, c, rr1, along


def middle_kernel(total_ref, all_ref, r0_ref, v1_ref, v2_ref, gx_ref, gy_ref, gz_ref, s_ref, part_ref, r2_ref, q1_ref, sums_ref):
    a0, a1, c, _, _ = first_scalars(total_ref)
    sums_ref[...] = jnp.zeros_like(sums_ref)
    mask = all_ref[MASK]
    beta = all_ref[BETA]

    @pl.loop(0, 2 * LEV)
    def _(p):
        v1 = v1_ref[p]
        q1 = c * v1 - a0 * v2_ref[p]
        r2 = r0_ref[p] - a0 * v1 - a1 * q1
        q1_ref[p] = q1
        r2_ref[p] = r2
        sums_ref[0] += folded(r2, r2)
        sums_ref[1] += folded(r2, q1)
        sums_ref[2] += folded(q1, q1)

    def at_level(level):
        return jnp.where(level == 0, beta, 0.0)

    @pl.loop(0, LEV)
    def _(level):
        for c, value in enumerate(apply_level(planes_of(r2_ref), level, gx_ref, gy_ref, gz_ref, mask, at_level(level))):
            p = c * LEV + level
            s_ref[p] = value
            sums_ref[3] += folded(value, r2_ref[p])
            sums_ref[4] += folded(value, value)
            sums_ref[5] += folded(value, q1_ref[p])

    @pl.loop(0, LEV)
    def _(level):
        for c, value in enumerate(apply_level(planes_of(q1_ref), level, gx_ref, gy_ref, gz_ref, mask, at_level(level))):
            sums_ref[6] += folded(value, q1_ref[c * LEV + level])

    @pl.loop(0, LEV)
    def _(level):
        for c, value in enumerate(apply_level(planes_of(s_ref), level, gx_ref, gy_ref, gz_ref, mask, at_level(level))):
            p = c * LEV + level
            sums_ref[7] += folded(value, s_ref[p])
            sums_ref[8] += folded(value, q1_ref[p])

    d = summed(sums_ref, 9)
    part_ref[...] = tile_of([(d[0], d[1]), (d[2], d[3]), (d[4], d[5]), (d[6], d[7]), (d[8], d[8])])


def end_kernel(first_ref, second_ref, all_ref, r0_ref, v1_ref, v2_ref, s_ref, velocity_ref, spread_ref):
    a0, a1, c, rr1, pq = first_scalars(first_ref)
    pair = lambda i: (second_ref[i : i + 1, 0:1], second_ref[i : i + 1, 64:65])
    (rr2, rq), (qq, rs), (ss, sq), (tq, su), (uq, _) = (pair(i) for i in range(5))
    b = rr2 / rr1
    p2q2 = rs + 2.0 * b * rq + b * b * pq
    a2 = rr2 / p2q2
    r2q2 = rs + b * rq
    q2q2 = ss + 2.0 * b * sq + b * b * qq
    rr3 = rr2 - 2.0 * a2 * r2q2 + a2 * a2 * q2q2
    b3 = rr3 / rr2
    q2t2 = su + 2.0 * b * uq + b * b * tq
    p3q3 = (
        rs
        - 2.0 * a2 * (ss + b * sq)
        + a2 * a2 * q2t2
        + 2.0 * b3 * (r2q2 - a2 * q2q2)
        + b3 * b3 * p2q2
    )
    a3 = rr3 / p3q3
    of_p2 = a2 + a3 * b3
    of_r2 = of_p2 + a3
    of_p1 = of_p2 * b + a1
    of_s = -(a3 * a2)
    of_q1 = of_s * b - of_r2 * a1
    of_r0 = a0 + of_p1 * c + of_r2
    of_v1 = of_q1 * c - of_p1 * a0 - of_r2 * a0
    of_v2 = -(of_q1 * a0)

    means = []
    for k in range(2):
        mean = jnp.zeros((TALL, LONG), F32)
        for level in range(LEV):
            p = k * LEV + level
            value = all_ref[p] + of_r0 * r0_ref[p] + of_v1 * v1_ref[p] + of_v2 * v2_ref[p] + of_s * s_ref[p]
            velocity_ref[p] = value[:ROWS, :COLS]
            mean = mean + value
        means.append(all_ref[THICK] * (mean * (1.0 / LEV)))
    spread = 0.5 * (next_row(means[0]) - last_row(means[0])) + 0.5 * (next_col(means[1]) - last_col(means[1]))
    spread_ref[...] = spread[:ROWS, :COLS]


def solve(padded, most):
    block = jax.ShapeDtypeStruct((2 * LEV, TALL, LONG), F32)
    tile = jax.ShapeDtypeStruct((8, 128), F32)
    level = jax.ShapeDtypeStruct((LEV, TALL, LONG), F32)
    room = pltpu.CompilerParams(vmem_limit_bytes=56 << 20)
    r0, v1, v2, gx, gy, gz, part = pl.pallas_call(
        begin_kernel,
        name="begin",
        out_shape=(block, block, block, level, level, jax.ShapeDtypeStruct((LEV + 1, TALL, LONG), F32), tile),
        in_specs=[VM] * 2,
        out_specs=(VM,) * 7,
        scratch_shapes=[pltpu.VMEM((LEV, TALL, LONG), F32), pltpu.VMEM((4, 8, COLS), F32)],
        compiler_params=room,
    )(padded, most)
    first = total(part, "total_first", 1)
    s, part = pl.pallas_call(
        middle_kernel,
        name="middle",
        out_shape=(block, tile),
        in_specs=[VM] * 8,
        out_specs=(VM,) * 2,
        scratch_shapes=[pltpu.VMEM((2 * LEV, TALL, LONG), F32)] * 2 + [pltpu.VMEM((9, 8, COLS), F32)],
        compiler_params=room,
    )(first, padded, r0, v1, v2, gx, gy, gz)
    second = total(part, "total_second", 6)
    velocity, spread = pl.pallas_call(
        end_kernel,
        name="end",
        out_shape=(
            jax.ShapeDtypeStruct((2 * LEV, ROWS, COLS), F32),
            jax.ShapeDtypeStruct((ROWS, COLS), F32),
        ),
        in_specs=[VM] * 7,
        out_specs=(VM,) * 2,
        compiler_params=room,
    )(first, second, padded, r0, v1, v2, s)
    return velocity.reshape(2, LEV, ROWS, COLS), spread, first[7, 0]


def on_device(
    velocity_start,
    stiffness,
    beta,
    ice_mask,
    thickness,
    bed,
    land_smb,
    elev_class,
    correlation_cols,
    correlation_weights,
):
    rows, cols = bed.shape
    own_table = land_smb.reshape(-1, 128)

    def turn(number):
        return route(
            jnp.full((1,), number, jnp.int32), correlation_cols, elev_class, correlation_weights
        )

    def balance_and_weights(send, cell, got, swap):
        denom, found = owner(own_table, got)
        return scatter(cell, send, swap(found)), denom

    def plain_swap(array):
        return lax.all_to_all(array, ("ty", "tx"), 0, 0, tiled=True)

    send, cell, most = turn(0)
    got = exchange(send, "to_owner", 2)
    smb_ice, denom = balance_and_weights(send, cell, got, lambda a: exchange(a, "from_owner", 3))

    padded = with_halo(velocity_start, stiffness, ice_mask, thickness, bed, beta)
    velocity, spread, most = solve(padded, most)
    turns = ((most.astype(jnp.int32) + SLOTS - 1) // SLOTS).astype(jnp.int32)

    def more_balance(carry):
        number, smb, weights = carry
        send, cell, _ = turn(number)
        add_smb, add_weights = balance_and_weights(send, cell, plain_swap(send), plain_swap)
        return number + 1, smb + add_smb, weights + add_weights

    def unfinished(carry):
        return carry[0] < turns

    _, smb_ice, denom = lax.while_loop(unfinished, more_balance, (jnp.int32(1), smb_ice, denom))
    surface = bed + thickness + 0.5 * (smb_ice.reshape(rows, cols) - spread)
    surface_rows = surface.reshape(-1, 128)
    numer = scatter(got, got, exchange(gather(surface_rows, cell), "to_land", 4))

    def more_numer(carry):
        number, numer = carry
        send, cell, _ = turn(number)
        got = plain_swap(send)
        return number + 1, numer + scatter(got, got, plain_swap(gather(surface_rows, cell)))

    _, numer = lax.while_loop(unfinished, more_numer, (jnp.int32(1), numer))
    used = own_table.shape[0]
    land_surface = (numer[:used] / (denom[:used] + 1.0)).reshape(land_smb.shape)
    return (velocity, surface, land_surface)


def solution(mesh):
    every = ("ty", "tx")
    return jax.shard_map(
        on_device,
        mesh=mesh,
        in_specs=(
            P(None, None, "ty", "tx"),
            P(None, "ty", "tx"),
            P("ty", "tx"),
            P("ty", "tx"),
            P("ty", "tx"),
            P("ty", "tx"),
            P(None, every),
            P("ty", "tx"),
            P(None, "ty", "tx"),
            P(None, "ty", "tx"),
        ),
        out_specs=(P(None, None, "ty", "tx"), P("ty", "tx"), P(None, every)),
        check_vma=False,
    )
```

```python
import functools
import jax
import jax.numpy as jnp
from jax import lax
from jax.experimental import pallas as pl
from jax.experimental.pallas import tpu as pltpu
from jax.sharding import PartitionSpec as P

MESH = pl.DeviceIdType.MESH
F32 = jnp.float32
BF = jnp.bfloat16
VM = pl.BlockSpec(memory_space=pltpu.VMEM)
SM = pl.BlockSpec(memory_space=pltpu.SMEM)
SLOTS = 128
HIGH = 64
NT = (((1,), (1,)), ((), ()))


def parts(x, count):
    out = []
    for _ in range(count):
        top = x.astype(BF)
        out.append(top)
        x = x - top.astype(F32)
    return out


def is_row(size, row):
    return lax.broadcasted_iota(jnp.int32, (size, row.shape[1]), 0) == row


def hot(size, row):
    return jnp.where(is_row(size, row), 1.0, 0.0).astype(BF)


def route_kernel(peers, turn_ref, cols_ref, class_ref, weights_ref, send_ref, cell_ref, most_ref, left_ref, right_ref, total_ref):
    width = cols_ref.shape[1]
    step = 8
    before = lax.broadcasted_iota(jnp.int32, (width, 2 * width), 0) < lax.broadcasted_iota(
        jnp.int32, (width, 2 * width), 1
    )
    ahead = jnp.where(before, 1.0, 0.0).astype(BF)
    first = 0 if turn_ref is None else turn_ref[0] * SLOTS
    most = jnp.zeros((peers, width), F32)
    for k in range(4):
        total_ref[...] = jnp.zeros_like(total_ref)

        def body(g, base):
            at = pl.multiple_of(k * 32 + g * step, step)
            cols = cols_ref[pl.ds(at, step), :]
            kind = class_ref[pl.ds(pl.multiple_of(g * step, step), step), :]
            dest = cols >> 9
            lane = lax.broadcasted_iota(jnp.int32, cols.shape, 1)
            row = lax.broadcasted_iota(jnp.int32, cols.shape, 0) + g * step
            whole = (kind * 4 + ((cols >> 7) & 3), cols & 127, (lane >> 7) * 32 + row, lane & 127)
            fields = [v.astype(F32) for v in whole]
            w = weights_ref[pl.ds(at, step), :]
            w_top = w.astype(BF).astype(F32)
            fields += [w_top, w - w_top]
            for r in range(step):
                one = slice(r, r + 1)
                mask = is_row(peers, dest[one])
                picked = jnp.where(mask, 1.0, 0.0).astype(BF)
                counts = jnp.dot(picked, ahead, preferred_element_type=F32)
                rank = jnp.sum(jnp.where(mask, counts[:, :width] + base, 0.0), axis=0, keepdims=True)
                base = base + counts[:, width:]
                span = pl.ds(r * width, width)
                for f, value in enumerate(fields):
                    left_ref[f * peers : (f + 1) * peers, span] = picked * value[one].astype(BF)
                right_ref[:, span] = hot(SLOTS, rank.astype(jnp.int32) - first)
            total_ref[...] += lax.dot_general(left_ref[...], right_ref[...], NT, preferred_element_type=F32)
            return base

        base = lax.fori_loop(0, 32 // step, body, jnp.zeros((peers, width), F32))
        f = [total_ref[i * peers : (i + 1) * peers, :] for i in range(6)]
        send_ref[:, k, :] = f[0] * 128.0 + f[1]
        cell_ref[:, k, :] = f[2] * 128.0 + f[3]
        send_ref[:, 4 + k, :] = f[4] + f[5]
        most = jnp.maximum(most, base)
    most_ref[...] = jnp.broadcast_to(jnp.max(most, keepdims=True), most_ref.shape)


def route(turn, cols, kind, weights, peers=128):
    rows, width = 4 * cols.shape[1], cols.shape[2]
    return pl.pallas_call(
        functools.partial(route_kernel, peers),
        name="route",
        out_shape=(
            jax.ShapeDtypeStruct((peers, 8, SLOTS), F32),
            jax.ShapeDtypeStruct((peers, 4, SLOTS), F32),
            jax.ShapeDtypeStruct((8, 128), F32),
        ),
        in_specs=[SM, VM, VM, VM],
        out_specs=(VM, VM, VM),
        scratch_shapes=[
            pltpu.VMEM((6 * peers, 8 * width), BF),
            pltpu.VMEM((SLOTS, 8 * width), BF),
            pltpu.VMEM((6 * peers, SLOTS), F32),
        ],
        compiler_params=pltpu.CompilerParams(vmem_limit_bytes=48 << 20),
    )(turn, cols.reshape(rows, width), kind, weights.reshape(rows, width))


def spots(where):
    at = where.astype(jnp.int32)
    return at >> 7, at & 127


def table_terms(table):
    padded = jnp.concatenate([table, jnp.zeros((HIGH - table.shape[0], 128), F32)], axis=0) if table.shape[0] < HIGH else table
    return jnp.concatenate([p.astype(F32) for p in parts(padded, 3)], axis=0).T.astype(BF)


def look_up(terms, high, low_masks):
    stacked = jnp.concatenate([high] * 3, axis=0)
    found = jnp.dot(terms, stacked, preferred_element_type=F32)
    return jnp.sum(jnp.where(low_masks, found, 0.0), axis=0, keepdims=True)


def across(pieces):
    return jnp.concatenate(pieces, axis=1)


def add_in(total_ref, values, high, low):
    both = jnp.concatenate([high * v.astype(BF) for v in values], axis=0)
    total_ref[...] += lax.dot_general(both, low, NT, preferred_element_type=F32)


GROUP = 4


def flat_rows(tiles):
    return [tiles[s, k : k + 1, :] for s in range(tiles.shape[0]) for k in range(4)]


def owner_group(g, got_ref, terms_ref, total_ref, back_ref):
    tile = got_ref[pl.ds(g * GROUP, GROUP), :, :]
    high, low = spots(tile[:, :4, :])
    w = across(flat_rows(tile[:, 4:, :]))
    high_hot = hot(HIGH, across(flat_rows(high)))
    low_mask = is_row(128, across(flat_rows(low)))
    low_hot = jnp.where(low_mask, 1.0, 0.0).astype(BF)
    w_top = w.astype(BF).astype(F32)
    add_in(total_ref, (w_top, w - w_top), high_hot, low_hot)
    found = look_up(terms_ref[...], high_hot, low_mask)
    put_rows(back_ref, g, found)


def put_rows(out_ref, g, found):
    for s in range(GROUP):
        for k in range(4):
            i = s * 4 + k
            out_ref[g * GROUP + s, k : k + 1, :] = found[:, i * 128 : (i + 1) * 128]


def gather_group(g, terms_ref, where_ref, out_ref):
    high, low = spots(where_ref[pl.ds(g * GROUP, GROUP), :, :])
    found = look_up(
        terms_ref[...], hot(HIGH, across(flat_rows(high))), is_row(128, across(flat_rows(low)))
    )
    put_rows(out_ref, g, found)


def scatter_group(g, where_ref, weights_ref, values_ref, total_ref):
    span = pl.ds(g * GROUP, GROUP)
    high, low = spots(where_ref[span, :4, :])
    v = across(flat_rows(weights_ref[span, 4:, :] * values_ref[span, :, :]))
    v_top = v.astype(BF).astype(F32)
    add_in(
        total_ref,
        (v_top, v - v_top),
        hot(HIGH, across(flat_rows(high))),
        hot(128, across(flat_rows(low))),
    )


def owner_kernel(table_ref, got_ref, denom_ref, back_ref, terms_ref, total_ref):
    terms_ref[...] = table_terms(table_ref[...])
    total_ref[...] = jnp.zeros_like(total_ref)

    @pl.loop(0, got_ref.shape[0] // GROUP)
    def _(g):
        owner_group(g, got_ref, terms_ref, total_ref, back_ref)

    denom_ref[...] = total_ref[:HIGH, :] + total_ref[HIGH:, :]


def owner(table, got):
    peers = got.shape[0]
    return pl.pallas_call(
        owner_kernel,
        name="owner",
        out_shape=(jax.ShapeDtypeStruct((HIGH, 128), F32), jax.ShapeDtypeStruct((peers, 4, SLOTS), F32)),
        in_specs=[VM, VM],
        out_specs=(VM, VM),
        scratch_shapes=[pltpu.VMEM((128, 3 * HIGH), BF), pltpu.VMEM((2 * HIGH, 128), F32)],
        compiler_params=pltpu.CompilerParams(vmem_limit_bytes=48 << 20),
    )(table, got)


def gather_kernel(table_ref, where_ref, out_ref, terms_ref):
    terms_ref[...] = table_terms(table_ref[...])

    @pl.loop(0, where_ref.shape[0] // GROUP)
    def _(g):
        gather_group(g, terms_ref, where_ref, out_ref)


def gather(table, where):
    return pl.pallas_call(
        gather_kernel,
        name="pick",
        out_shape=jax.ShapeDtypeStruct(where.shape, F32),
        in_specs=[VM, VM],
        out_specs=VM,
        scratch_shapes=[pltpu.VMEM((128, 3 * HIGH), BF)],
        compiler_params=pltpu.CompilerParams(vmem_limit_bytes=48 << 20),
    )(table, where)


def scatter_kernel(where_ref, weights_ref, values_ref, out_ref, total_ref):
    total_ref[...] = jnp.zeros_like(total_ref)

    @pl.loop(0, where_ref.shape[0] // GROUP)
    def _(g):
        scatter_group(g, where_ref, weights_ref, values_ref, total_ref)

    out_ref[...] = total_ref[:HIGH, :] + total_ref[HIGH:, :]


def scatter(where, weights, values):
    return pl.pallas_call(
        scatter_kernel,
        name="put",
        out_shape=jax.ShapeDtypeStruct((HIGH, 128), F32),
        in_specs=[VM, VM, VM],
        out_specs=VM,
        scratch_shapes=[pltpu.VMEM((2 * HIGH, 128), F32)],
        compiler_params=pltpu.CompilerParams(vmem_limit_bytes=48 << 20),
    )(where, weights, values)


def place():
    wide = lax.axis_size("tx")
    return lax.axis_index("ty") * wide + lax.axis_index("tx"), lax.axis_size("ty") * wide


def at(peer):
    wide = lax.axis_size("tx")
    return (peer // wide, peer % wide)


LEV = 10
ROWS, COLS = 32, 256
TALL, LONG = 48, 384
RIM = 8
PLANES = 3 * LEV + 4
MASK, THICK, BED, BETA = range(3 * LEV, PLANES)
PACKS = 3
ALL_ROWS = pl.ds(0, ROWS)


def pack_halo(fields, all_ref, left_ref, right_ref, each):
    vel_ref, stiff_ref, mask_ref, thick_ref, bed_ref, beta_ref = fields
    lane = lax.broadcasted_iota(jnp.int32, (ROWS, 128), 1)
    left = [jnp.zeros((ROWS, 128), F32)] * PACKS
    right = [jnp.zeros((ROWS, 128), F32)] * PACKS
    for p in range(PLANES):
        if p < 2 * LEV:
            plane = vel_ref[p]
        elif p < 3 * LEV:
            plane = stiff_ref[p - 2 * LEV]
        elif p == MASK:
            plane = mask_ref[...].astype(F32)
        else:
            plane = {THICK: thick_ref, BED: bed_ref, BETA: beta_ref}[p][...]
        all_ref[p, :ROWS, :COLS] = plane
        pack, k = p // 16, p % 16
        here = (lane >= RIM * k) & (lane < RIM * (k + 1))
        first, last = plane[:, :128], plane[:, COLS - 128 :]
        left[pack] = jnp.where(here, pltpu.roll(first, RIM * k, 1) if k else first, left[pack])
        turn = (RIM * k + RIM) % 128
        right[pack] = jnp.where(here, pltpu.roll(last, turn, 1) if turn else last, right[pack])
        each(p)
    for i in range(PACKS):
        left_ref[i] = left[i]
        right_ref[i] = right[i]


def halo_copies(all_ref, left_ref, right_ref, from_right, from_left, out_sem, in_sem):
    y, x = lax.axis_index("ty"), lax.axis_index("tx")
    tall, wide = lax.axis_size("ty"), lax.axis_size("tx")
    around = [(a, b) for a in (-1, 0, 1) for b in (-1, 0, 1) if (a, b) != (0, 0)]
    copies = []
    for i, (a, b) in enumerate(around):
        rows = {-1: pl.ds(0, RIM), 0: ALL_ROWS, 1: pl.ds(ROWS - RIM, RIM)}[a]
        there = {-1: pl.ds(ROWS, RIM), 0: ALL_ROWS, 1: pl.ds(TALL - RIM, RIM)}[a]
        if b == 0:
            ends = all_ref.at[:, rows, pl.ds(0, COLS)], all_ref.at[:, there, pl.ds(0, COLS)]
        elif b < 0:
            ends = left_ref.at[:, rows, :], from_right.at[:, there, :]
        else:
            ends = right_ref.at[:, rows, :], from_left.at[:, there, :]
        device = ((y + a + tall) % tall, (x + b + wide) % wide)
        copies.append(
            pltpu.make_async_remote_copy(
                *ends, out_sem.at[i], in_sem.at[i], device_id=device, device_id_type=MESH
            )
        )
    return copies


def unpack_halo(all_ref, from_right, from_left):
    y, x = lax.axis_index("ty"), lax.axis_index("tx")
    tall, wide = lax.axis_size("ty"), lax.axis_size("tx")
    row = lax.broadcasted_iota(jnp.int32, (TALL, 128), 0)
    lane = lax.broadcasted_iota(jnp.int32, (TALL, 128), 1)
    inside = (row < ROWS) | ((row < ROWS + RIM) & (y < tall - 1)) | ((row >= TALL - RIM) & (y > 0))
    on_right = inside & (lane < RIM) & (x < wide - 1)
    on_left = inside & (lane >= 128 - RIM) & (x > 0)
    rights = [from_right[i] for i in range(PACKS)]
    lefts = [from_left[i] for i in range(PACKS)]
    for p in range(PLANES):
        pack, k = p // 16, p % 16
        to_right = pltpu.roll(rights[pack], 128 - RIM * k, 1) if k else rights[pack]
        turn = (128 - RIM - RIM * k) % 128
        to_left = pltpu.roll(lefts[pack], turn, 1) if turn else lefts[pack]
        all_ref[p, :, COLS:] = jnp.where(on_right, to_right, jnp.where(on_left, to_left, 0.0))

    @pl.when(y == tall - 1)
    def _():
        all_ref[:, ROWS : ROWS + RIM, :COLS] = jnp.zeros((PLANES, RIM, COLS), F32)

    @pl.when(y == 0)
    def _():
        all_ref[:, TALL - RIM :, :COLS] = jnp.zeros((PLANES, RIM, COLS), F32)


def next_row(a):
    return pltpu.roll(a, a.shape[0] - 1, 0)


def last_row(a):
    return pltpu.roll(a, 1, 0)


def next_col(a):
    return pltpu.roll(a, a.shape[1] - 1, 1)


def last_col(a):
    return pltpu.roll(a, 1, 1)


def folded(a, b):
    inner = a[:ROWS, :COLS] * b[:ROWS, :COLS]
    return inner[0:8] + inner[8:16] + inner[16:24] + inner[24:32]


def apply_level(source, level, gx_ref, gy_ref, gz_ref, mask, friction):
    gx, gy = gx_ref[level], gy_ref[level]
    over, under = gz_ref[level + 1], gz_ref[level]
    upper = jnp.minimum(level + 1, LEV - 1)
    lower = jnp.maximum(level - 1, 0)
    results = []
    for c, (along_x, along_y) in enumerate(((2.0, 0.5), (0.5, 2.0))):
        w = source(c, level)
        held = mask * w
        flow_x = gx * (held - next_row(held))
        flow_y = gy * (held - next_col(held))
        value = along_x * (flow_x - last_row(flow_x)) + along_y * (flow_y - last_col(flow_y))
        value = value + over * (held - mask * source(c, upper)) + under * (held - mask * source(c, lower))
        value = value + friction * held
        results.append(jnp.where(mask > 0.0, value, w))
    return results


def planes_of(ref):
    return lambda c, level: ref[c * LEV + level]


def tile_of(pairs, last=None):
    lane = lax.broadcasted_iota(jnp.int32, (1, 128), 1)
    rows = [jnp.where(lane < 64, a, b) for a, b in pairs]
    rows += [jnp.zeros((1, 128), F32)] * (7 - len(rows))
    rows.append(jnp.zeros((1, 128), F32) if last is None else last)
    return jnp.concatenate(rows, axis=0)


def summed(sums_ref, count):
    return [jnp.sum(sums_ref[i], keepdims=True) for i in range(count)]


def begin(each, all_ref, most_ref, r0_ref, v1_ref, v2_ref, gx_ref, gy_ref, gz_ref, part_ref, mu_ref, sums_ref):
    sums_ref[...] = jnp.zeros_like(sums_ref)
    mask = all_ref[MASK]
    beta = all_ref[BETA]

    @pl.loop(0, LEV)
    def _(level):
        each(level)
        upper = jnp.minimum(level + 1, LEV - 1)
        u, v = all_ref[level], all_ref[LEV + level]
        grad_xx = 0.5 * (next_row(u) - last_row(u))
        grad_yy = 0.5 * (next_col(v) - last_col(v))
        cross = 0.5 * (next_col(u) - last_col(u)) + 0.5 * (next_row(v) - last_row(v))
        shear_x = all_ref[upper] - u
        shear_y = all_ref[LEV + upper] - v
        rate = grad_xx * grad_xx + grad_yy * grad_yy + grad_xx * grad_yy
        rate = rate + 0.25 * (cross * cross) + 0.25 * (shear_x * shear_x + shear_y * shear_y)
        base = rate + 0.1
        root = jnp.exp(jnp.log(base) * (-1.0 / 3.0))
        root = root * (4.0 - base * (root * root * root)) * (1.0 / 3.0)
        mu_ref[level] = all_ref[2 * LEV + level] * root

    gz_ref[0] = jnp.zeros((TALL, LONG), F32)
    gz_ref[LEV] = jnp.zeros((TALL, LONG), F32)

    @pl.loop(0, LEV)
    def _(level):
        mu = mu_ref[level]
        gx_ref[level] = mu + next_row(mu)
        gy_ref[level] = mu + next_col(mu)

    @pl.loop(1, LEV)
    def _(level):
        gz_ref[level] = mu_ref[level - 1] + mu_ref[level]

    s0 = all_ref[BED] + all_ref[THICK]
    force = -(mask * all_ref[THICK])
    drive = (force * (0.5 * (next_row(s0) - last_row(s0))), force * (0.5 * (next_col(s0) - last_col(s0))))

    def at_level(level):
        return jnp.where(level == 0, beta, 0.0)

    @pl.loop(0, LEV)
    def _(level):
        for c, value in enumerate(apply_level(planes_of(all_ref), level, gx_ref, gy_ref, gz_ref, mask, at_level(level))):
            r = drive[c] - value
            r0_ref[c * LEV + level] = r
            sums_ref[0] += folded(r, r)

    @pl.loop(0, LEV)
    def _(level):
        for c, value in enumerate(apply_level(planes_of(r0_ref), level, gx_ref, gy_ref, gz_ref, mask, at_level(level))):
            v1_ref[c * LEV + level] = value
            sums_ref[1] += folded(value, r0_ref[c * LEV + level])
            sums_ref[2] += folded(value, value)

    @pl.loop(0, LEV)
    def _(level):
        for c, value in enumerate(apply_level(planes_of(v1_ref), level, gx_ref, gy_ref, gz_ref, mask, at_level(level))):
            v2_ref[c * LEV + level] = value
            sums_ref[3] += folded(value, v1_ref[c * LEV + level])

    part_ref[...] = tile_of([(s, s) for s in summed(sums_ref, 4)], most_ref[:1, :])


def first_scalars(total_ref):
    m0, m1, m2, m3 = (total_ref[i : i + 1, 0:1] for i in range(4))
    a0 = m0 / m1
    rr1 = a0 * a0 * m2 - m0
    b1 = rr1 / m0
    c = 1.0 + b1
    along = c * c * m1 - 2.0 * c * a0 * m2 + a0 * a0 * m3
    a1 = rr1 / along
    return a0, a1, c, rr1, along


def middle(total_ref, all_ref, r0_ref, v1_ref, v2_ref, gx_ref, gy_ref, gz_ref, s_ref, part_ref, r2_ref, q1_ref, sums_ref):
    a0, a1, c, _, _ = first_scalars(total_ref)
    sums_ref[...] = jnp.zeros_like(sums_ref)
    mask = all_ref[MASK]
    beta = all_ref[BETA]

    @pl.loop(0, 2 * LEV)
    def _(p):
        v1 = v1_ref[p]
        q1 = c * v1 - a0 * v2_ref[p]
        r2 = r0_ref[p] - a0 * v1 - a1 * q1
        q1_ref[p] = q1
        r2_ref[p] = r2
        sums_ref[0] += folded(r2, r2)
        sums_ref[1] += folded(r2, q1)
        sums_ref[2] += folded(q1, q1)

    def at_level(level):
        return jnp.where(level == 0, beta, 0.0)

    @pl.loop(0, LEV)
    def _(level):
        for c, value in enumerate(apply_level(planes_of(r2_ref), level, gx_ref, gy_ref, gz_ref, mask, at_level(level))):
            p = c * LEV + level
            s_ref[p] = value
            sums_ref[3] += folded(value, r2_ref[p])
            sums_ref[4] += folded(value, value)
            sums_ref[5] += folded(value, q1_ref[p])

    @pl.loop(0, LEV)
    def _(level):
        for c, value in enumerate(apply_level(planes_of(q1_ref), level, gx_ref, gy_ref, gz_ref, mask, at_level(level))):
            sums_ref[6] += folded(value, q1_ref[c * LEV + level])

    @pl.loop(0, LEV)
    def _(level):
        for c, value in enumerate(apply_level(planes_of(s_ref), level, gx_ref, gy_ref, gz_ref, mask, at_level(level))):
            p = c * LEV + level
            sums_ref[7] += folded(value, s_ref[p])
            sums_ref[8] += folded(value, q1_ref[p])

    d = summed(sums_ref, 9)
    part_ref[...] = tile_of([(d[0], d[1]), (d[2], d[3]), (d[4], d[5]), (d[6], d[7]), (d[8], d[8])])


def end(first_ref, second_ref, all_ref, r0_ref, v1_ref, v2_ref, s_ref, velocity_ref):
    a0, a1, c, rr1, pq = first_scalars(first_ref)
    pair = lambda i: (second_ref[i : i + 1, 0:1], second_ref[i : i + 1, 64:65])
    (rr2, rq), (qq, rs), (ss, sq), (tq, su), (uq, _) = (pair(i) for i in range(5))
    b = rr2 / rr1
    p2q2 = rs + 2.0 * b * rq + b * b * pq
    a2 = rr2 / p2q2
    r2q2 = rs + b * rq
    q2q2 = ss + 2.0 * b * sq + b * b * qq
    rr3 = rr2 - 2.0 * a2 * r2q2 + a2 * a2 * q2q2
    b3 = rr3 / rr2
    q2t2 = su + 2.0 * b * uq + b * b * tq
    p3q3 = (
        rs
        - 2.0 * a2 * (ss + b * sq)
        + a2 * a2 * q2t2
        + 2.0 * b3 * (r2q2 - a2 * q2q2)
        + b3 * b3 * p2q2
    )
    a3 = rr3 / p3q3
    of_p2 = a2 + a3 * b3
    of_r2 = of_p2 + a3
    of_p1 = of_p2 * b + a1
    of_s = -(a3 * a2)
    of_q1 = of_s * b - of_r2 * a1
    of_r0 = a0 + of_p1 * c + of_r2
    of_v1 = of_q1 * c - of_p1 * a0 - of_r2 * a0
    of_v2 = -(of_q1 * a0)

    means = []
    for k in range(2):
        mean = jnp.zeros((TALL, LONG), F32)
        for level in range(LEV):
            p = k * LEV + level
            value = all_ref[p] + of_r0 * r0_ref[p] + of_v1 * v1_ref[p] + of_v2 * v2_ref[p] + of_s * s_ref[p]
            velocity_ref[p] = value[:ROWS, :COLS]
            mean = mean + value
        means.append(all_ref[THICK] * (mean * (1.0 / LEV)))
    spread = 0.5 * (next_row(means[0]) - last_row(means[0])) + 0.5 * (next_col(means[1]) - last_col(means[1]))
    return spread[:ROWS, :COLS]


def joined(tiles):
    row = lax.broadcasted_iota(jnp.int32, tiles.shape[1:], 0)
    return jnp.where(row < 7, jnp.sum(tiles, axis=0), jnp.max(tiles, axis=0))


class Total:
    def __init__(self, part_ref, near_ref, half_ref, far_ref, sems):
        y, x = lax.axis_index("ty"), lax.axis_index("tx")
        tall, wide = lax.axis_size("ty"), lax.axis_size("tx")
        core, chip = x % 2, x // 2
        near, far = tall * 2, wide // 2
        self.me, self.chip = y * 2 + core, chip
        ids = [(self.me + i) % near for i in range(1, near)]
        self.near_devices = [(i // 2, chip * 2 + i % 2) for i in ids]
        self.far_devices = [(y, ((chip + i) % far) * 2 + core) for i in range(1, far)]
        self.part, self.near, self.half, self.far, self.sems = part_ref, near_ref, half_ref, far_ref, sems

    def send(self, source, target, place, devices, first):
        for device in devices:
            pltpu.make_async_remote_copy(
                source, target.at[place], self.sems.at[first], self.sems.at[first + 1],
                device_id=device, device_id_type=MESH,
            ).start()
        target[pl.ds(place, 1)] = source[...][None]

    def wait(self, target, devices, first):
        whole = pl.ds(0, len(devices))
        pltpu.make_async_remote_copy(
            target.at[whole], target.at[whole], self.sems.at[first], self.sems.at[first + 1],
            device_id=devices[0], device_id_type=MESH,
        ).wait()

    def start(self):
        self.send(self.part, self.near, self.me, self.near_devices, 0)

    def turn(self):
        self.wait(self.near, self.near_devices, 0)
        self.half[...] = joined(self.near[...])
        self.send(self.half, self.far, self.chip, self.far_devices, 2)

    def finish(self, sum_ref):
        self.wait(self.far, self.far_devices, 2)
        sum_ref[...] = joined(self.far[...])


def send_block(source, target, peer, me, sems):
    pltpu.make_async_remote_copy(
        source.at[peer], target.at[me], sems.at[0], sems.at[1], device_id=at(peer), device_id_type=MESH
    ).start()


def await_blocks(source, target, me, peers, sems):
    target[pl.ds(me, 1)] = source[pl.ds(me, 1)]
    others = pl.ds(0, peers - 1)
    pltpu.make_async_remote_copy(
        source.at[others], target.at[others], sems.at[0], sems.at[1],
        device_id=at((me + 1) % peers), device_id_type=MESH,
    ).wait()


def send_group(source, target, g, me, sems):
    for s in range(GROUP):
        peer = g * GROUP + s

        @pl.when(peer != me)
        def _():
            send_block(source, target, peer, me, sems)


def whole_kernel(
    vel_ref, stiff_ref, mask_ref, thick_ref, bed_ref, beta_ref, table_ref, cols_ref, class_ref, weights_ref,
    velocity_ref, surface_ref, land_ref, spread_ref, first_ref,
    all_ref, left_ref, right_ref, from_right, from_left,
    send_ref, cell_ref, most_ref, route_left, route_right, route_total,
    got_ref, found_ref, back_ref, value_ref, last_ref,
    r0_ref, v1_ref, v2_ref, r2_ref, q1_ref, s_ref, gx_ref, gy_ref, gz_ref, mu_ref,
    sums_ref, part1_ref, near1_ref, half1_ref, far1_ref, part2_ref, near2_ref, half2_ref, far2_ref, second_ref,
    terms_ref, surface_terms, denom_ref, smb_ref, numer_ref,
    halo_out, halo_in, total1_sem, total2_sem, to_owner, from_owner, to_land,
):
    me, peers = place()
    groups = peers // GROUP
    barrier = pltpu.get_barrier_semaphore()

    def greet(p):
        for step in range(4 * p + 1, min(4 * p + 5, 128)):
            pl.semaphore_signal(barrier, inc=1, device_id=at((me + step) % peers), device_id_type=MESH)

    pack_halo((vel_ref, stiff_ref, mask_ref, thick_ref, bed_ref, beta_ref), all_ref, left_ref, right_ref, greet)
    pl.semaphore_wait(barrier, peers - 1)
    halo = halo_copies(all_ref, left_ref, right_ref, from_right, from_left, halo_out, halo_in)
    for copy in halo:
        copy.start()
    route_kernel(
        peers, None, cols_ref, class_ref, weights_ref, send_ref, cell_ref, most_ref, route_left, route_right, route_total
    )
    for copy in halo:
        copy.wait()
    unpack_halo(all_ref, from_right, from_left)

    def to_owners(level):
        for i in range(13):
            step = level * 13 + i + 1

            @pl.when(step < peers)
            def _():
                send_block(send_ref, got_ref, (me + step) % peers, me, to_owner)

    begin(to_owners, all_ref, most_ref, r0_ref, v1_ref, v2_ref, gx_ref, gy_ref, gz_ref, part1_ref, mu_ref, sums_ref)
    total1 = Total(part1_ref, near1_ref, half1_ref, far1_ref, total1_sem)
    total1.start()
    await_blocks(send_ref, got_ref, me, peers, to_owner)
    terms_ref[...] = table_terms(table_ref[...])
    denom_ref[...] = jnp.zeros_like(denom_ref)

    def own_group(g):
        @pl.when(g > 0)
        def _():
            send_group(found_ref, back_ref, g - 1, me, from_owner)

        owner_group(g, got_ref, terms_ref, denom_ref, found_ref)

    pl.loop(0, groups // 2)(own_group)
    total1.turn()
    pl.loop(groups // 2, groups)(own_group)
    total1.finish(first_ref)
    send_group(found_ref, back_ref, groups - 1, me, from_owner)
    middle(first_ref, all_ref, r0_ref, v1_ref, v2_ref, gx_ref, gy_ref, gz_ref, s_ref, part2_ref, r2_ref, q1_ref, sums_ref)
    total2 = Total(part2_ref, near2_ref, half2_ref, far2_ref, total2_sem)
    total2.start()
    await_blocks(found_ref, back_ref, me, peers, from_owner)
    smb_ref[...] = jnp.zeros_like(smb_ref)

    def cell_group(g):
        scatter_group(g, cell_ref, send_ref, back_ref, smb_ref)

    pl.loop(0, groups // 2)(cell_group)
    total2.turn()
    pl.loop(groups // 2, groups)(cell_group)
    total2.finish(second_ref)
    spread = end(first_ref, second_ref, all_ref, r0_ref, v1_ref, v2_ref, s_ref, velocity_ref)
    spread_ref[...] = spread
    smb = smb_ref[:HIGH, :] + smb_ref[HIGH:, :]
    halves = []
    for h in range(2):
        side = slice(h * 128, (h + 1) * 128)
        half = bed_ref[:, side] + thick_ref[:, side] + 0.5 * (smb[h * ROWS : (h + 1) * ROWS] - spread[:, side])
        surface_ref[:, side] = half
        halves.append(half)
    surface_terms[...] = table_terms(jnp.concatenate(halves, axis=0))

    @pl.loop(0, groups)
    def _(g):
        @pl.when(g > 0)
        def _():
            send_group(value_ref, last_ref, g - 1, me, to_land)

        gather_group(g, surface_terms, cell_ref, value_ref)

    numer_ref[...] = jnp.zeros_like(numer_ref)
    send_group(value_ref, last_ref, groups - 1, me, to_land)
    await_blocks(value_ref, last_ref, me, peers, to_land)

    @pl.loop(0, groups)
    def _(g):
        scatter_group(g, got_ref, got_ref, last_ref, numer_ref)

    used = land_ref.shape[0]
    numer = numer_ref[:used, :] + numer_ref[HIGH : HIGH + used, :]
    denom = denom_ref[:used, :] + denom_ref[HIGH : HIGH + used, :]
    land_ref[...] = numer / (denom + 1.0)


def whole(velocity, stiffness, mask, thickness, bed, beta, table, cols, kind, weights):
    tall, wide = lax.axis_size("ty"), lax.axis_size("tx")
    peers = tall * wide
    shape = lambda *dims: jax.ShapeDtypeStruct(dims, F32)
    room = lambda *dims: pltpu.VMEM(dims, F32)
    block, level = (2 * LEV, TALL, LONG), (LEV, TALL, LONG)
    sum_room = [room(8, 128), room(2 * tall, 8, 128), room(8, 128), room(wide // 2, 8, 128)]
    pair = pltpu.SemaphoreType.DMA((2,))
    return pl.pallas_call(
        whole_kernel,
        name="whole",
        out_shape=(shape(2 * LEV, ROWS, COLS), shape(ROWS, COLS), shape(*table.shape), shape(ROWS, COLS), shape(8, 128)),
        in_specs=[VM] * 10,
        out_specs=(VM,) * 5,
        scratch_shapes=[
            room(PLANES, TALL, LONG), room(PACKS, ROWS, 128), room(PACKS, ROWS, 128),
            room(PACKS, TALL, 128), room(PACKS, TALL, 128),
            room(peers, 8, SLOTS), room(peers, 4, SLOTS), room(8, 128),
            pltpu.VMEM((6 * peers, 8 * COLS), BF), pltpu.VMEM((SLOTS, 8 * COLS), BF), room(6 * peers, SLOTS),
            room(peers, 8, SLOTS), room(peers, 4, SLOTS), room(peers, 4, SLOTS), room(peers, 4, SLOTS), room(peers, 4, SLOTS),
            room(*block), room(*block), room(*block), room(*block), room(*block), room(*block),
            room(*level), room(*level), room(LEV + 1, TALL, LONG), room(*level),
            room(9, 8, COLS), *sum_room, *sum_room, room(8, 128),
            pltpu.VMEM((128, 3 * HIGH), BF), pltpu.VMEM((128, 3 * HIGH), BF),
            room(2 * HIGH, 128), room(2 * HIGH, 128), room(2 * HIGH, 128),
            pltpu.SemaphoreType.DMA((8,)), pltpu.SemaphoreType.DMA((8,)),
            pltpu.SemaphoreType.DMA((4,)), pltpu.SemaphoreType.DMA((4,)), pair, pair, pair,
        ],
        compiler_params=pltpu.CompilerParams(
            collective_id=1, has_side_effects=True, vmem_limit_bytes=60 << 20
        ),
    )(
        velocity.reshape(2 * LEV, ROWS, COLS), stiffness, mask, thickness, bed, beta, table,
        cols.reshape(4 * ROWS, COLS), kind, weights.reshape(4 * ROWS, COLS),
    )


def on_device(
    velocity_start,
    stiffness,
    beta,
    ice_mask,
    thickness,
    bed,
    land_smb,
    elev_class,
    correlation_cols,
    correlation_weights,
):
    table = land_smb.reshape(-1, 128)
    velocity, surface, land, spread, first = whole(
        velocity_start, stiffness, ice_mask, thickness, bed, beta, table, correlation_cols, elev_class, correlation_weights
    )
    turns = ((first[7, 0].astype(jnp.int32) + SLOTS - 1) // SLOTS).astype(jnp.int32)

    def swap(array):
        return lax.all_to_all(array, ("ty", "tx"), 0, 0, tiled=True)

    def turn(number):
        return route(
            jnp.full((1,), number, jnp.int32), correlation_cols, elev_class, correlation_weights
        )

    def unfinished(carry):
        return carry[0] < turns

    def in_turns():
        def balance(carry):
            number, smb, denom = carry
            send, cell, _ = turn(number)
            add_denom, found = owner(table, swap(send))
            return number + 1, smb + scatter(cell, send, swap(found)), denom + add_denom

        none = jnp.zeros((HIGH, 128), F32)
        _, smb, denom = lax.while_loop(unfinished, balance, (jnp.int32(0), none, none))
        halves = [
            bed[:, s] + thickness[:, s] + 0.5 * (smb[h * ROWS : (h + 1) * ROWS] - spread[:, s])
            for h, s in enumerate((slice(0, 128), slice(128, 256)))
        ]
        rows = jnp.concatenate(halves, axis=0)

        def raised(carry):
            number, numer = carry
            send, cell, _ = turn(number)
            got = swap(send)
            return number + 1, numer + scatter(got, got, swap(gather(rows, cell)))

        _, numer = lax.while_loop(unfinished, raised, (jnp.int32(0), none))
        used = table.shape[0]
        return jnp.concatenate(halves, axis=1), numer[:used] / (denom[:used] + 1.0)

    surface, land = lax.cond(turns > 1, in_turns, lambda: (surface, land))
    return velocity.reshape(velocity_start.shape), surface, land.reshape(land_smb.shape)


def solution(mesh):
    every = ("ty", "tx")
    return jax.shard_map(
        on_device,
        mesh=mesh,
        in_specs=(
            P(None, None, "ty", "tx"),
            P(None, "ty", "tx"),
            P("ty", "tx"),
            P("ty", "tx"),
            P("ty", "tx"),
            P("ty", "tx"),
            P(None, every),
            P("ty", "tx"),
            P(None, "ty", "tx"),
            P(None, "ty", "tx"),
        ),
        out_specs=(P(None, None, "ty", "tx"), P("ty", "tx"), P(None, every)),
        check_vma=False,
    )
```

```python
import functools
import jax
import jax.numpy as jnp
from jax import lax
from jax.experimental import pallas as pl
from jax.experimental.pallas import tpu as pltpu
from jax.sharding import PartitionSpec as P

MESH = pl.DeviceIdType.MESH
F32 = jnp.float32
BF = jnp.bfloat16
VM = pl.BlockSpec(memory_space=pltpu.VMEM)
SM = pl.BlockSpec(memory_space=pltpu.SMEM)
SLOTS = 128
HIGH = 64
NT = (((1,), (1,)), ((), ()))


def parts(x, count):
    out = []
    for _ in range(count):
        top = x.astype(BF)
        out.append(top)
        x = x - top.astype(F32)
    return out


def is_row(size, row):
    return lax.broadcasted_iota(jnp.int32, (size, row.shape[1]), 0) == row


def hot(size, row):
    rows = lax.broadcasted_iota(jnp.int32, (size, row.shape[1]), 0).astype(F32).astype(BF)
    return jnp.where(rows == row.astype(F32).astype(BF), jnp.ones((), BF), jnp.zeros((), BF))


def route_kernel(peers, turn_ref, cols_ref, class_ref, weights_ref, send_ref, cell_ref, most_ref, left_ref, right_ref, total_ref, stack_ref, counts_ref):
    width = cols_ref.shape[1]
    step, half = 8, peers // 2
    before = lax.broadcasted_iota(jnp.int32, (width, width), 0) < lax.broadcasted_iota(
        jnp.int32, (width, width), 1
    )
    ahead = jnp.where(before, 1.0, 0.0).astype(BF)
    first = 0 if turn_ref is None else turn_ref[0] * SLOTS
    most = jnp.zeros((peers, 128), F32)
    for k in range(4):
        total_ref[...] = jnp.zeros_like(total_ref)

        def body(g, base):
            at = pl.multiple_of(k * 32 + g * step, step)
            cols = cols_ref[pl.ds(at, step), :]
            kind = class_ref[pl.ds(pl.multiple_of(g * step, step), step), :]
            dest = cols >> 9
            lane = lax.broadcasted_iota(jnp.int32, cols.shape, 1)
            row = lax.broadcasted_iota(jnp.int32, cols.shape, 0) + g * step
            whole = (((cols >> 7) & 3) * 10 + kind, cols & 127, (lane >> 7) * 32 + row, lane & 127)
            fields = [v.astype(F32) for v in whole]
            w = weights_ref[pl.ds(at, step), :]
            w_top = w.astype(BF).astype(F32)
            fields += [w_top, w - w_top]
            for r in range(step):
                stack_ref[r * peers : (r + 1) * peers, :] = hot(peers, dest[r : r + 1])
            counts_ref[...] = jnp.dot(stack_ref[...], ahead, preferred_element_type=F32)
            for r in range(step):
                one, span = slice(r, r + 1), pl.ds(r * width, width)
                picked = stack_ref[r * peers : (r + 1) * peers, :]
                counts = counts_ref[r * peers : (r + 1) * peers, :]
                so_far = jnp.concatenate([base] * (width // 128), axis=1)
                rank = jnp.sum(picked.astype(F32) * (counts + so_far), axis=0, keepdims=True)
                last = counts[:, width - 1 :] + picked[:, width - 128 :].astype(F32)[:, 127:]
                base = base + jnp.broadcast_to(last, (peers, 128))
                slot = rank.astype(jnp.int32) - first
                kept = (slot >= 0) & (slot < SLOTS)
                slot = jnp.where(kept, slot + jnp.where(dest[one] < half, 0, SLOTS), -1)
                right_ref[:, span] = hot(2 * SLOTS, slot)
                folded_in = picked[:half] + picked[half:]
                for f, value in enumerate(fields):
                    left_ref[f * half : (f + 1) * half, span] = folded_in * value[one].astype(BF)
            total_ref[...] += lax.dot_general(left_ref[...], right_ref[...], NT, preferred_element_type=F32)
            return base

        base = lax.fori_loop(0, 32 // step, body, jnp.zeros((peers, 128), F32))
        f = [
            jnp.concatenate([total_ref[i * half : (i + 1) * half, j * SLOTS : (j + 1) * SLOTS] for j in range(2)], axis=0)
            for i in range(6)
        ]
        send_ref[:, k, :] = f[0] * 128.0 + f[1]
        cell_ref[:, k, :] = f[2] * 128.0 + f[3]
        send_ref[:, 4 + k, :] = f[4] + f[5]
        most = jnp.maximum(most, base)
    most_ref[...] = jnp.broadcast_to(jnp.max(most, keepdims=True), most_ref.shape)


def route(turn, cols, kind, weights, peers=128):
    rows, width = 4 * cols.shape[1], cols.shape[2]
    return pl.pallas_call(
        functools.partial(route_kernel, peers),
        name="route",
        out_shape=(
            jax.ShapeDtypeStruct((peers, 8, SLOTS), F32),
            jax.ShapeDtypeStruct((peers, 4, SLOTS), F32),
            jax.ShapeDtypeStruct((8, 128), F32),
        ),
        in_specs=[SM, VM, VM, VM],
        out_specs=(VM, VM, VM),
        scratch_shapes=[
            pltpu.VMEM((3 * peers, 8 * width), BF),
            pltpu.VMEM((2 * SLOTS, 8 * width), BF),
            pltpu.VMEM((3 * peers, 2 * SLOTS), F32),
            pltpu.VMEM((8 * peers, width), BF),
            pltpu.VMEM((8 * peers, width), F32),
        ],
        compiler_params=pltpu.CompilerParams(vmem_limit_bytes=48 << 20),
    )(turn, cols.reshape(rows, width), kind, weights.reshape(rows, width))


def spots(where):
    at = where.astype(jnp.int32)
    return at >> 7, at & 127


def table_terms(table, count):
    return jnp.concatenate([p.astype(F32) for p in parts(table, count)], axis=0).T.astype(BF)


def look_up(terms, rows, at):
    high = hot(rows, at >> 7)
    found = jnp.dot(terms, jnp.concatenate([high] * (terms.shape[1] // rows), axis=0), preferred_element_type=F32)
    rows = 128
    while rows > 8:
        rows //= 2
        upper = jnp.broadcast_to(at & rows, (8, at.shape[1])) > 0
        found = jnp.concatenate(
            [jnp.where(upper, found[rows + i : rows + i + 8], found[i : i + 8]) for i in range(0, rows, 8)], axis=0
        )
    return jnp.sum(jnp.where(is_row(8, at & 7), found, 0.0), axis=0, keepdims=True)


def across(pieces):
    return jnp.concatenate(pieces, axis=1)


def add_in(total_ref, values, high, low):
    both = jnp.concatenate([high * v.astype(BF) for v in values], axis=0)
    total_ref[...] += lax.dot_general(both, low, NT, preferred_element_type=F32)


GROUP = 16


def flat_rows(tiles):
    return [tiles[s, k : k + 1, :] for s in range(tiles.shape[0]) for k in range(4)]


def put_rows(out_ref, g, found):
    for s in range(GROUP):
        for k in range(4):
            i = s * 4 + k
            out_ref[g * GROUP + s, k : k + 1, :] = found[:, i * 128 : (i + 1) * 128]


def owner_group(g, got_ref, terms_ref, total_ref, back_ref):
    tile = got_ref[pl.ds(g * GROUP, GROUP), :, :]
    at_all = across(flat_rows(tile[:, :4, :].astype(jnp.int32)))
    w = across(flat_rows(tile[:, 4:, :]))
    w_top = w.astype(BF).astype(F32)
    add_in(total_ref, (w_top, w - w_top), hot(HIGH, at_all >> 7), hot(128, at_all & 127))
    put_rows(back_ref, g, look_up(terms_ref[...], 40, at_all))


def gather_group(g, terms_ref, where_ref, out_ref):
    at_all = across(flat_rows(where_ref[pl.ds(g * GROUP, GROUP), :, :].astype(jnp.int32)))
    put_rows(out_ref, g, look_up(terms_ref[...], HIGH, at_all))


def scatter_group(g, where_ref, weights_ref, values_ref, total_ref):
    span = pl.ds(g * GROUP, GROUP)
    at_all = across(flat_rows(where_ref[span, :4, :].astype(jnp.int32)))
    v = across(flat_rows(weights_ref[span, 4:, :] * values_ref[span, :, :]))
    v_top = v.astype(BF).astype(F32)
    add_in(total_ref, (v_top, v - v_top), hot(HIGH, at_all >> 7), hot(128, at_all & 127))


def owner_kernel(table_ref, got_ref, denom_ref, back_ref, terms_ref, total_ref):
    terms_ref[...] = table_terms(table_ref[...], 3)
    total_ref[...] = jnp.zeros_like(total_ref)

    @pl.loop(0, got_ref.shape[0] // GROUP)
    def _(g):
        owner_group(g, got_ref, terms_ref, total_ref, back_ref)

    denom_ref[...] = total_ref[:HIGH, :] + total_ref[HIGH:, :]


def owner(table, got):
    peers = got.shape[0]
    return pl.pallas_call(
        owner_kernel,
        name="owner",
        out_shape=(jax.ShapeDtypeStruct((HIGH, 128), F32), jax.ShapeDtypeStruct((peers, 4, SLOTS), F32)),
        in_specs=[VM, VM],
        out_specs=(VM, VM),
        scratch_shapes=[pltpu.VMEM((128, 120), BF), pltpu.VMEM((2 * HIGH, 128), F32)],
        compiler_params=pltpu.CompilerParams(vmem_limit_bytes=48 << 20),
    )(table, got)


def gather_kernel(table_ref, where_ref, out_ref, terms_ref):
    terms_ref[...] = table_terms(table_ref[...], 2)

    @pl.loop(0, where_ref.shape[0] // GROUP)
    def _(g):
        gather_group(g, terms_ref, where_ref, out_ref)


def gather(table, where):
    return pl.pallas_call(
        gather_kernel,
        name="pick",
        out_shape=jax.ShapeDtypeStruct(where.shape, F32),
        in_specs=[VM, VM],
        out_specs=VM,
        scratch_shapes=[pltpu.VMEM((128, 128), BF)],
        compiler_params=pltpu.CompilerParams(vmem_limit_bytes=48 << 20),
    )(table, where)


def scatter_kernel(where_ref, weights_ref, values_ref, out_ref, total_ref):
    total_ref[...] = jnp.zeros_like(total_ref)

    @pl.loop(0, where_ref.shape[0] // GROUP)
    def _(g):
        scatter_group(g, where_ref, weights_ref, values_ref, total_ref)

    out_ref[...] = total_ref[:HIGH, :] + total_ref[HIGH:, :]


def scatter(where, weights, values):
    return pl.pallas_call(
        scatter_kernel,
        name="put",
        out_shape=jax.ShapeDtypeStruct((HIGH, 128), F32),
        in_specs=[VM, VM, VM],
        out_specs=VM,
        scratch_shapes=[pltpu.VMEM((2 * HIGH, 128), F32)],
        compiler_params=pltpu.CompilerParams(vmem_limit_bytes=48 << 20),
    )(where, weights, values)


def place():
    wide = lax.axis_size("tx")
    return lax.axis_index("ty") * wide + lax.axis_index("tx"), lax.axis_size("ty") * wide


def at(peer):
    wide = lax.axis_size("tx")
    return (peer // wide, peer % wide)


def meet(me, peers):
    barrier = pltpu.get_barrier_semaphore()

    @pl.loop(1, peers)
    def _(step):
        pl.semaphore_signal(barrier, inc=1, device_id=at((me + step) % peers), device_id_type=MESH)

    pl.semaphore_wait(barrier, peers - 1)


def exchange_kernel(send_ref, got_ref, out_sem, in_sem, own_sem):
    me, peers = place()
    own = pltpu.make_async_copy(send_ref.at[me], got_ref.at[me], own_sem)
    own.start()
    meet(me, peers)

    @pl.loop(1, peers)
    def _(step):
        peer = (me + step) % peers
        pltpu.make_async_remote_copy(
            send_ref.at[peer], got_ref.at[me], out_sem, in_sem, device_id=at(peer), device_id_type=MESH
        ).start()

    own.wait()
    others = pl.ds(0, peers - 1)
    whole = pltpu.make_async_remote_copy(
        send_ref.at[others], got_ref.at[others], out_sem, in_sem, device_id=at((me + 1) % peers), device_id_type=MESH
    )
    whole.wait()


def exchange(send, name, number):
    return pl.pallas_call(
        exchange_kernel,
        name=name,
        out_shape=jax.ShapeDtypeStruct(send.shape, send.dtype),
        in_specs=[VM],
        out_specs=VM,
        scratch_shapes=[pltpu.SemaphoreType.DMA] * 3,
        compiler_params=pltpu.CompilerParams(collective_id=number, has_side_effects=True),
    )(send)


LEV = 10
ROWS, COLS = 32, 256
TALL, LONG = 48, 384
RIM = 8
PLANES = 3 * LEV + 4
MASK, THICK, BED, BETA = range(3 * LEV, PLANES)
PACKS = 3
ALL_ROWS = pl.ds(0, ROWS)


def pack_halo(fields, all_ref, left_ref, right_ref, each):
    vel_ref, stiff_ref, mask_ref, thick_ref, bed_ref, beta_ref = fields
    lane = lax.broadcasted_iota(jnp.int32, (ROWS, 128), 1)
    left = [jnp.zeros((ROWS, 128), F32)] * PACKS
    right = [jnp.zeros((ROWS, 128), F32)] * PACKS
    for p in range(PLANES):
        if p < 2 * LEV:
            plane = vel_ref[p]
        elif p < 3 * LEV:
            plane = stiff_ref[p - 2 * LEV]
        elif p == MASK:
            plane = mask_ref[...].astype(F32)
        else:
            plane = {THICK: thick_ref, BED: bed_ref, BETA: beta_ref}[p][...]
        all_ref[p, :ROWS, :COLS] = plane
        pack, k = p // 16, p % 16
        here = (lane >= RIM * k) & (lane < RIM * (k + 1))
        first, last = plane[:, :128], plane[:, COLS - 128 :]
        left[pack] = jnp.where(here, pltpu.roll(first, RIM * k, 1) if k else first, left[pack])
        turn = (RIM * k + RIM) % 128
        right[pack] = jnp.where(here, pltpu.roll(last, turn, 1) if turn else last, right[pack])
        each(p)
    for i in range(PACKS):
        left_ref[i] = left[i]
        right_ref[i] = right[i]


def halo_copies(all_ref, left_ref, right_ref, from_right, from_left, out_sem, in_sem):
    y, x = lax.axis_index("ty"), lax.axis_index("tx")
    tall, wide = lax.axis_size("ty"), lax.axis_size("tx")
    around = [(a, b) for a in (-1, 0, 1) for b in (-1, 0, 1) if (a, b) != (0, 0)]
    copies = []
    for i, (a, b) in enumerate(around):
        rows = {-1: pl.ds(0, RIM), 0: ALL_ROWS, 1: pl.ds(ROWS - RIM, RIM)}[a]
        there = {-1: pl.ds(ROWS, RIM), 0: ALL_ROWS, 1: pl.ds(TALL - RIM, RIM)}[a]
        if b == 0:
            ends = all_ref.at[:, rows, pl.ds(0, COLS)], all_ref.at[:, there, pl.ds(0, COLS)]
        elif b < 0:
            ends = left_ref.at[:, rows, :], from_right.at[:, there, :]
        else:
            ends = right_ref.at[:, rows, :], from_left.at[:, there, :]
        device = ((y + a + tall) % tall, (x + b + wide) % wide)
        copies.append(
            pltpu.make_async_remote_copy(
                *ends, out_sem.at[i], in_sem.at[i], device_id=device, device_id_type=MESH
            )
        )
    return copies


def unpack_halo(all_ref, from_right, from_left):
    y, x = lax.axis_index("ty"), lax.axis_index("tx")
    tall, wide = lax.axis_size("ty"), lax.axis_size("tx")
    row = lax.broadcasted_iota(jnp.int32, (TALL, 128), 0)
    lane = lax.broadcasted_iota(jnp.int32, (TALL, 128), 1)
    inside = (row < ROWS) | ((row < ROWS + RIM) & (y < tall - 1)) | ((row >= TALL - RIM) & (y > 0))
    on_right = inside & (lane < RIM) & (x < wide - 1)
    on_left = inside & (lane >= 128 - RIM) & (x > 0)
    rights = [from_right[i] for i in range(PACKS)]
    lefts = [from_left[i] for i in range(PACKS)]
    for p in range(PLANES):
        pack, k = p // 16, p % 16
        to_right = pltpu.roll(rights[pack], 128 - RIM * k, 1) if k else rights[pack]
        turn = (128 - RIM - RIM * k) % 128
        to_left = pltpu.roll(lefts[pack], turn, 1) if turn else lefts[pack]
        all_ref[p, :, COLS:] = jnp.where(on_right, to_right, jnp.where(on_left, to_left, 0.0))

    @pl.when(y == tall - 1)
    def _():
        all_ref[:, ROWS : ROWS + RIM, :COLS] = jnp.zeros((PLANES, RIM, COLS), F32)

    @pl.when(y == 0)
    def _():
        all_ref[:, TALL - RIM :, :COLS] = jnp.zeros((PLANES, RIM, COLS), F32)


def next_row(a):
    return pltpu.roll(a, a.shape[0] - 1, 0)


def last_row(a):
    return pltpu.roll(a, 1, 0)


def next_col(a):
    return pltpu.roll(a, a.shape[1] - 1, 1)


def last_col(a):
    return pltpu.roll(a, 1, 1)


def folded(a, b):
    inner = a[:ROWS, :COLS] * b[:ROWS, :COLS]
    return inner[0:8] + inner[8:16] + inner[16:24] + inner[24:32]


def apply_level(source, level, gx_ref, gy_ref, gz_ref, mask, friction):
    gx, gy = gx_ref[level], gy_ref[level]
    over, under = gz_ref[level + 1], gz_ref[level]
    upper = jnp.minimum(level + 1, LEV - 1)
    lower = jnp.maximum(level - 1, 0)
    results = []
    for c, (along_x, along_y) in enumerate(((2.0, 0.5), (0.5, 2.0))):
        w = source(c, level)
        held = mask * w
        flow_x = gx * (held - next_row(held))
        flow_y = gy * (held - next_col(held))
        value = along_x * (flow_x - last_row(flow_x)) + along_y * (flow_y - last_col(flow_y))
        value = value + over * (held - mask * source(c, upper)) + under * (held - mask * source(c, lower))
        value = value + friction * held
        results.append(jnp.where(mask > 0.0, value, w))
    return results


def planes_of(ref):
    return lambda c, level: ref[c * LEV + level]


def tile_of(pairs, last=None):
    lane = lax.broadcasted_iota(jnp.int32, (1, 128), 1)
    rows = [jnp.where(lane < 64, a, b) for a, b in pairs]
    rows += [jnp.zeros((1, 128), F32)] * (7 - len(rows))
    rows.append(jnp.zeros((1, 128), F32) if last is None else last)
    return jnp.concatenate(rows, axis=0)


def summed(sums_ref, count):
    return [jnp.sum(sums_ref[i], keepdims=True) for i in range(count)]


def begin(each, all_ref, most_ref, r0_ref, v1_ref, v2_ref, gx_ref, gy_ref, gz_ref, part_ref, mu_ref, sums_ref):
    sums_ref[...] = jnp.zeros_like(sums_ref)
    mask = all_ref[MASK]
    beta = all_ref[BETA]

    @pl.loop(0, LEV)
    def _(level):
        each(level)
        upper = jnp.minimum(level + 1, LEV - 1)
        u, v = all_ref[level], all_ref[LEV + level]
        grad_xx = 0.5 * (next_row(u) - last_row(u))
        grad_yy = 0.5 * (next_col(v) - last_col(v))
        cross = 0.5 * (next_col(u) - last_col(u)) + 0.5 * (next_row(v) - last_row(v))
        shear_x = all_ref[upper] - u
        shear_y = all_ref[LEV + upper] - v
        rate = grad_xx * grad_xx + grad_yy * grad_yy + grad_xx * grad_yy
        rate = rate + 0.25 * (cross * cross) + 0.25 * (shear_x * shear_x + shear_y * shear_y)
        base = rate + 0.1
        root = jnp.exp(jnp.log(base) * (-1.0 / 3.0))
        root = root * (4.0 - base * (root * root * root)) * (1.0 / 3.0)
        mu_ref[level] = all_ref[2 * LEV + level] * root

    gz_ref[0] = jnp.zeros((TALL, LONG), F32)
    gz_ref[LEV] = jnp.zeros((TALL, LONG), F32)

    @pl.loop(0, LEV)
    def _(level):
        mu = mu_ref[level]
        gx_ref[level] = mu + next_row(mu)
        gy_ref[level] = mu + next_col(mu)

    @pl.loop(1, LEV)
    def _(level):
        gz_ref[level] = mu_ref[level - 1] + mu_ref[level]

    s0 = all_ref[BED] + all_ref[THICK]
    force = -(mask * all_ref[THICK])
    drive = (force * (0.5 * (next_row(s0) - last_row(s0))), force * (0.5 * (next_col(s0) - last_col(s0))))

    def at_level(level):
        return jnp.where(level == 0, beta, 0.0)

    @pl.loop(0, LEV)
    def _(level):
        for c, value in enumerate(apply_level(planes_of(all_ref), level, gx_ref, gy_ref, gz_ref, mask, at_level(level))):
            r = drive[c] - value
            r0_ref[c * LEV + level] = r
            sums_ref[0] += folded(r, r)

    @pl.loop(0, LEV)
    def _(level):
        for c, value in enumerate(apply_level(planes_of(r0_ref), level, gx_ref, gy_ref, gz_ref, mask, at_level(level))):
            v1_ref[c * LEV + level] = value
            sums_ref[1] += folded(value, r0_ref[c * LEV + level])
            sums_ref[2] += folded(value, value)

    @pl.loop(0, LEV)
    def _(level):
        for c, value in enumerate(apply_level(planes_of(v1_ref), level, gx_ref, gy_ref, gz_ref, mask, at_level(level))):
            v2_ref[c * LEV + level] = value
            sums_ref[3] += folded(value, v1_ref[c * LEV + level])

    part_ref[...] = tile_of([(s, s) for s in summed(sums_ref, 4)], most_ref[:1, :])


def first_scalars(total_ref):
    m0, m1, m2, m3 = (total_ref[i : i + 1, 0:1] for i in range(4))
    a0 = m0 / m1
    rr1 = a0 * a0 * m2 - m0
    b1 = rr1 / m0
    c = 1.0 + b1
    along = c * c * m1 - 2.0 * c * a0 * m2 + a0 * a0 * m3
    a1 = rr1 / along
    return a0, a1, c, rr1, along


def middle(total_ref, all_ref, r0_ref, v1_ref, v2_ref, gx_ref, gy_ref, gz_ref, s_ref, part_ref, r2_ref, q1_ref, sums_ref):
    a0, a1, c, _, _ = first_scalars(total_ref)
    sums_ref[...] = jnp.zeros_like(sums_ref)
    mask = all_ref[MASK]
    beta = all_ref[BETA]

    @pl.loop(0, 2 * LEV)
    def _(p):
        v1 = v1_ref[p]
        q1 = c * v1 - a0 * v2_ref[p]
        r2 = r0_ref[p] - a0 * v1 - a1 * q1
        q1_ref[p] = q1
        r2_ref[p] = r2
        sums_ref[0] += folded(r2, r2)
        sums_ref[1] += folded(r2, q1)
        sums_ref[2] += folded(q1, q1)

    def at_level(level):
        return jnp.where(level == 0, beta, 0.0)

    @pl.loop(0, LEV)
    def _(level):
        for c, value in enumerate(apply_level(planes_of(r2_ref), level, gx_ref, gy_ref, gz_ref, mask, at_level(level))):
            p = c * LEV + level
            s_ref[p] = value
            sums_ref[3] += folded(value, r2_ref[p])
            sums_ref[4] += folded(value, value)
            sums_ref[5] += folded(value, q1_ref[p])

    @pl.loop(0, LEV)
    def _(level):
        for c, value in enumerate(apply_level(planes_of(q1_ref), level, gx_ref, gy_ref, gz_ref, mask, at_level(level))):
            sums_ref[6] += folded(value, q1_ref[c * LEV + level])

    @pl.loop(0, LEV)
    def _(level):
        for c, value in enumerate(apply_level(planes_of(s_ref), level, gx_ref, gy_ref, gz_ref, mask, at_level(level))):
            p = c * LEV + level
            sums_ref[7] += folded(value, s_ref[p])
            sums_ref[8] += folded(value, q1_ref[p])

    d = summed(sums_ref, 9)
    part_ref[...] = tile_of([(d[0], d[1]), (d[2], d[3]), (d[4], d[5]), (d[6], d[7]), (d[8], d[8])])


def end(first_ref, second_ref, all_ref, r0_ref, v1_ref, v2_ref, s_ref, velocity_ref):
    a0, a1, c, rr1, pq = first_scalars(first_ref)
    pair = lambda i: (second_ref[i : i + 1, 0:1], second_ref[i : i + 1, 64:65])
    (rr2, rq), (qq, rs), (ss, sq), (tq, su), (uq, _) = (pair(i) for i in range(5))
    b = rr2 / rr1
    p2q2 = rs + 2.0 * b * rq + b * b * pq
    a2 = rr2 / p2q2
    r2q2 = rs + b * rq
    q2q2 = ss + 2.0 * b * sq + b * b * qq
    rr3 = rr2 - 2.0 * a2 * r2q2 + a2 * a2 * q2q2
    b3 = rr3 / rr2
    q2t2 = su + 2.0 * b * uq + b * b * tq
    p3q3 = (
        rs
        - 2.0 * a2 * (ss + b * sq)
        + a2 * a2 * q2t2
        + 2.0 * b3 * (r2q2 - a2 * q2q2)
        + b3 * b3 * p2q2
    )
    a3 = rr3 / p3q3
    of_p2 = a2 + a3 * b3
    of_r2 = of_p2 + a3
    of_p1 = of_p2 * b + a1
    of_s = -(a3 * a2)
    of_q1 = of_s * b - of_r2 * a1
    of_r0 = a0 + of_p1 * c + of_r2
    of_v1 = of_q1 * c - of_p1 * a0 - of_r2 * a0
    of_v2 = -(of_q1 * a0)

    means = []
    for k in range(2):
        mean = jnp.zeros((TALL, LONG), F32)
        for level in range(LEV):
            p = k * LEV + level
            value = all_ref[p] + of_r0 * r0_ref[p] + of_v1 * v1_ref[p] + of_v2 * v2_ref[p] + of_s * s_ref[p]
            velocity_ref[p] = value[:ROWS, :COLS]
            mean = mean + value
        means.append(all_ref[THICK] * (mean * (1.0 / LEV)))
    spread = 0.5 * (next_row(means[0]) - last_row(means[0])) + 0.5 * (next_col(means[1]) - last_col(means[1]))
    return spread[:ROWS, :COLS]


def joined(tiles):
    row = lax.broadcasted_iota(jnp.int32, tiles.shape[1:], 0)
    return jnp.where(row < 7, jnp.sum(tiles, axis=0), jnp.max(tiles, axis=0))


class Total:
    def __init__(self, part_ref, near_ref, half_ref, far_ref, sems):
        y, x = lax.axis_index("ty"), lax.axis_index("tx")
        tall, wide = lax.axis_size("ty"), lax.axis_size("tx")
        core, chip = x % 2, x // 2
        near, far = tall * 2, wide // 2
        self.me, self.chip = y * 2 + core, chip
        ids = [(self.me + i) % near for i in range(1, near)]
        self.near_devices = [(i // 2, chip * 2 + i % 2) for i in ids]
        self.far_devices = [(y, ((chip + i) % far) * 2 + core) for i in range(1, far)]
        self.part, self.near, self.half, self.far, self.sems = part_ref, near_ref, half_ref, far_ref, sems

    def send(self, source, target, place, devices, first):
        for device in devices:
            pltpu.make_async_remote_copy(
                source, target.at[place], self.sems.at[first], self.sems.at[first + 1],
                device_id=device, device_id_type=MESH,
            ).start()
        target[pl.ds(place, 1)] = source[...][None]

    def wait(self, target, devices, first):
        whole = pl.ds(0, len(devices))
        pltpu.make_async_remote_copy(
            target.at[whole], target.at[whole], self.sems.at[first], self.sems.at[first + 1],
            device_id=devices[0], device_id_type=MESH,
        ).wait()

    def start(self):
        self.send(self.part, self.near, self.me, self.near_devices, 0)

    def turn(self):
        self.wait(self.near, self.near_devices, 0)
        self.half[...] = joined(self.near[...])
        self.send(self.half, self.far, self.chip, self.far_devices, 2)

    def finish(self, sum_ref):
        self.wait(self.far, self.far_devices, 2)
        sum_ref[...] = joined(self.far[...])


def send_block(source, target, peer, me, sems):
    pltpu.make_async_remote_copy(
        source.at[peer], target.at[me], sems.at[0], sems.at[1], device_id=at(peer), device_id_type=MESH
    ).start()


def await_blocks(source, target, me, peers, sems):
    target[pl.ds(me, 1)] = source[pl.ds(me, 1)]
    others = pl.ds(0, peers - 1)
    pltpu.make_async_remote_copy(
        source.at[others], target.at[others], sems.at[0], sems.at[1],
        device_id=at((me + 1) % peers), device_id_type=MESH,
    ).wait()


def send_group(source, target, g, me, sems):
    for s in range(GROUP):
        peer = g * GROUP + s

        @pl.when(peer != me)
        def _():
            send_block(source, target, peer, me, sems)


def whole_kernel(
    vel_ref, stiff_ref, mask_ref, thick_ref, bed_ref, beta_ref, table_ref, cols_ref, class_ref, weights_ref,
    velocity_ref, surface_ref, land_ref, spread_ref, fullest_ref,
    first_ref, all_ref, left_ref, right_ref, from_right, from_left,
    send_ref, cell_ref, most_ref, route_left, route_right, route_total, route_stack, route_counts,
    got_ref, found_ref, back_ref, value_ref, last_ref,
    r0_ref, v1_ref, v2_ref, r2_ref, q1_ref, s_ref, gx_ref, gy_ref, gz_ref, mu_ref,
    sums_ref, part1_ref, near1_ref, half1_ref, far1_ref, part2_ref, near2_ref, half2_ref, far2_ref, second_ref,
    terms_ref, surface_terms, denom_ref, smb_ref, numer_ref,
    halo_out, halo_in, total1_sem, total2_sem, to_owner, from_owner, to_land,
):
    me, peers = place()
    groups = peers // GROUP
    barrier = pltpu.get_barrier_semaphore()

    def greet(p):
        for step in range(4 * p + 1, min(4 * p + 5, 128)):
            pl.semaphore_signal(barrier, inc=1, device_id=at((me + step) % peers), device_id_type=MESH)

    pack_halo((vel_ref, stiff_ref, mask_ref, thick_ref, bed_ref, beta_ref), all_ref, left_ref, right_ref, greet)
    pl.semaphore_wait(barrier, peers - 1)
    halo = halo_copies(all_ref, left_ref, right_ref, from_right, from_left, halo_out, halo_in)
    for copy in halo:
        copy.start()
    route_kernel(
        peers, None, cols_ref, class_ref, weights_ref, send_ref, cell_ref, most_ref, route_left, route_right, route_total,
        route_stack, route_counts,
    )
    for copy in halo:
        copy.wait()
    unpack_halo(all_ref, from_right, from_left)

    def to_owners(level):
        for i in range(13):
            step = level * 13 + i + 1

            @pl.when(step < peers)
            def _():
                send_block(send_ref, got_ref, (me + step) % peers, me, to_owner)

    begin(to_owners, all_ref, most_ref, r0_ref, v1_ref, v2_ref, gx_ref, gy_ref, gz_ref, part1_ref, mu_ref, sums_ref)
    total1 = Total(part1_ref, near1_ref, half1_ref, far1_ref, total1_sem)
    total1.start()
    await_blocks(send_ref, got_ref, me, peers, to_owner)
    table = jnp.concatenate([table_ref[:, t * 128 : (t + 1) * 128] for t in range(4)], axis=0)
    terms_ref[...] = table_terms(table, 3)
    denom_ref[...] = jnp.zeros_like(denom_ref)

    def own_group(g):
        @pl.when(g > 0)
        def _():
            send_group(found_ref, back_ref, g - 1, me, from_owner)

        owner_group(g, got_ref, terms_ref, denom_ref, found_ref)

    pl.loop(0, groups // 2)(own_group)
    total1.turn()
    pl.loop(groups // 2, groups)(own_group)
    total1.finish(first_ref)
    fullest_ref[0, 0] = jnp.max(first_ref[7:8, :])
    send_group(found_ref, back_ref, groups - 1, me, from_owner)
    middle(first_ref, all_ref, r0_ref, v1_ref, v2_ref, gx_ref, gy_ref, gz_ref, s_ref, part2_ref, r2_ref, q1_ref, sums_ref)
    total2 = Total(part2_ref, near2_ref, half2_ref, far2_ref, total2_sem)
    total2.start()
    await_blocks(found_ref, back_ref, me, peers, from_owner)
    smb_ref[...] = jnp.zeros_like(smb_ref)

    def cell_group(g):
        scatter_group(g, cell_ref, send_ref, back_ref, smb_ref)

    pl.loop(0, groups // 2)(cell_group)
    total2.turn()
    pl.loop(groups // 2, groups)(cell_group)
    total2.finish(second_ref)
    spread = end(first_ref, second_ref, all_ref, r0_ref, v1_ref, v2_ref, s_ref, velocity_ref)
    spread_ref[...] = spread
    smb = smb_ref[:HIGH, :] + smb_ref[HIGH:, :]
    halves = []
    for h in range(2):
        side = slice(h * 128, (h + 1) * 128)
        half = bed_ref[:, side] + thick_ref[:, side] + 0.5 * (smb[h * ROWS : (h + 1) * ROWS] - spread[:, side])
        surface_ref[:, side] = half
        halves.append(half)
    surface_terms[...] = table_terms(jnp.concatenate(halves, axis=0), 2)

    @pl.loop(0, groups)
    def _(g):
        @pl.when(g > 0)
        def _():
            send_group(value_ref, last_ref, g - 1, me, to_land)

        gather_group(g, surface_terms, cell_ref, value_ref)

    numer_ref[...] = jnp.zeros_like(numer_ref)
    send_group(value_ref, last_ref, groups - 1, me, to_land)
    await_blocks(value_ref, last_ref, me, peers, to_land)

    @pl.loop(0, groups)
    def _(g):
        scatter_group(g, got_ref, got_ref, last_ref, numer_ref)

    classes = land_ref.shape[0]
    for t in range(4):
        numer, denom = (
            ref[t * classes : (t + 1) * classes, :] + ref[HIGH + t * classes : HIGH + (t + 1) * classes, :]
            for ref in (numer_ref, denom_ref)
        )
        land_ref[:, t * 128 : (t + 1) * 128] = numer / (denom + 1.0)


def whole(velocity, stiffness, mask, thickness, bed, beta, table, cols, kind, weights):
    tall, wide = lax.axis_size("ty"), lax.axis_size("tx")
    peers = tall * wide
    shape = lambda *dims: jax.ShapeDtypeStruct(dims, F32)
    room = lambda *dims: pltpu.VMEM(dims, F32)
    block, level = (2 * LEV, TALL, LONG), (LEV, TALL, LONG)
    sum_room = [room(8, 128), room(2 * tall, 8, 128), room(8, 128), room(wide // 2, 8, 128)]
    pair = pltpu.SemaphoreType.DMA((2,))
    return pl.pallas_call(
        whole_kernel,
        name="whole",
        out_shape=(shape(2 * LEV, ROWS, COLS), shape(ROWS, COLS), shape(*table.shape), shape(ROWS, COLS), shape(1, 1)),
        in_specs=[VM] * 10,
        out_specs=(VM,) * 4 + (SM,),
        scratch_shapes=[
            room(8, 128),
            room(PLANES, TALL, LONG), room(PACKS, ROWS, 128), room(PACKS, ROWS, 128),
            room(PACKS, TALL, 128), room(PACKS, TALL, 128),
            room(peers, 8, SLOTS), room(peers, 4, SLOTS), room(8, 128),
            pltpu.VMEM((3 * peers, 8 * COLS), BF), pltpu.VMEM((2 * SLOTS, 8 * COLS), BF), room(3 * peers, 2 * SLOTS),
            pltpu.VMEM((8 * peers, COLS), BF), room(8 * peers, COLS),
            room(peers, 8, SLOTS), room(peers, 4, SLOTS), room(peers, 4, SLOTS), room(peers, 4, SLOTS), room(peers, 4, SLOTS),
            room(*block), room(*block), room(*block), room(*block), room(*block), room(*block),
            room(*level), room(*level), room(LEV + 1, TALL, LONG), room(*level),
            room(9, 8, COLS), *sum_room, *sum_room, room(8, 128),
            pltpu.VMEM((128, 120), BF), pltpu.VMEM((128, 128), BF),
            room(2 * HIGH, 128), room(2 * HIGH, 128), room(2 * HIGH, 128),
            pltpu.SemaphoreType.DMA((8,)), pltpu.SemaphoreType.DMA((8,)),
            pltpu.SemaphoreType.DMA((4,)), pltpu.SemaphoreType.DMA((4,)), pair, pair, pair,
        ],
        compiler_params=pltpu.CompilerParams(
            collective_id=1, has_side_effects=True, vmem_limit_bytes=60 << 20
        ),
    )(
        velocity.reshape(2 * LEV, ROWS, COLS), stiffness, mask, thickness, bed, beta, table,
        cols.reshape(4 * ROWS, COLS), kind, weights.reshape(4 * ROWS, COLS),
    )


def on_device(
    velocity_start,
    stiffness,
    beta,
    ice_mask,
    thickness,
    bed,
    land_smb,
    elev_class,
    correlation_cols,
    correlation_weights,
):
    velocity, surface, land, spread, fullest = whole(
        velocity_start, stiffness, ice_mask, thickness, bed, beta, land_smb, correlation_cols, elev_class, correlation_weights
    )
    turns = ((fullest[0, 0].astype(jnp.int32) + SLOTS - 1) // SLOTS).astype(jnp.int32)


    def turn(number):
        return route(
            jnp.full((1,), number, jnp.int32), correlation_cols, elev_class, correlation_weights
        )

    def unfinished(carry):
        return carry[0] < turns

    def in_turns():
        table = jnp.concatenate([land_smb[:, t * 128 : (t + 1) * 128] for t in range(4)], axis=0)

        def balance(carry):
            number, smb, denom = carry
            send, cell, _ = turn(number)
            add_denom, found = owner(table, exchange(send, "more_to_owner", 2))
            return number + 1, smb + scatter(cell, send, exchange(found, "more_from_owner", 3)), denom + add_denom

        none = jnp.zeros((HIGH, 128), F32)
        _, smb, denom = lax.while_loop(unfinished, balance, (jnp.int32(0), none, none))
        halves = [
            bed[:, s] + thickness[:, s] + 0.5 * (smb[h * ROWS : (h + 1) * ROWS] - spread[:, s])
            for h, s in enumerate((slice(0, 128), slice(128, 256)))
        ]
        rows = jnp.concatenate(halves, axis=0)

        def raised(carry):
            number, numer = carry
            send, cell, _ = turn(number)
            got = exchange(send, "again_to_owner", 4)
            return number + 1, numer + scatter(got, got, exchange(gather(rows, cell), "again_to_land", 5))

        _, numer = lax.while_loop(unfinished, raised, (jnp.int32(0), none))
        ratio, classes = numer / (denom + 1.0), land_smb.shape[0]
        land = jnp.concatenate([ratio[t * classes : (t + 1) * classes] for t in range(4)], axis=1)
        return jnp.concatenate(halves, axis=1), land

    surface, land = lax.cond(turns > 1, in_turns, lambda: (surface, land))
    return velocity.reshape(velocity_start.shape), surface, land


def solution(mesh):
    every = ("ty", "tx")
    return jax.shard_map(
        on_device,
        mesh=mesh,
        in_specs=(
            P(None, None, "ty", "tx"),
            P(None, "ty", "tx"),
            P("ty", "tx"),
            P("ty", "tx"),
            P("ty", "tx"),
            P("ty", "tx"),
            P(None, every),
            P("ty", "tx"),
            P(None, "ty", "tx"),
            P(None, "ty", "tx"),
        ),
        out_specs=(P(None, None, "ty", "tx"), P("ty", "tx"), P(None, every)),
        check_vma=False,
    )
```

```python
import functools
import jax
import jax.numpy as jnp
from jax import lax
from jax.experimental import pallas as pl
from jax.experimental.pallas import tpu as pltpu
from jax.sharding import PartitionSpec as P

MESH = pl.DeviceIdType.MESH
F32 = jnp.float32
BF = jnp.bfloat16
VM = pl.BlockSpec(memory_space=pltpu.VMEM)
SM = pl.BlockSpec(memory_space=pltpu.SMEM)
SLOTS = 128
HIGH = 64
NT = (((1,), (1,)), ((), ()))


def parts(x, count):
    out = []
    for _ in range(count):
        top = x.astype(BF)
        out.append(top)
        x = x - top.astype(F32)
    return out


def is_row(size, row):
    return lax.broadcasted_iota(jnp.int32, (size, row.shape[1]), 0) == row


def hot(size, row):
    rows = lax.broadcasted_iota(jnp.int32, (size, row.shape[1]), 0).astype(F32).astype(BF)
    return jnp.where(rows == row.astype(F32).astype(BF), jnp.ones((), BF), jnp.zeros((), BF))


def route_kernel(peers, turn_ref, cols_ref, class_ref, weights_ref, send_ref, cell_ref, most_ref, left_ref, right_ref, total_ref, stack_ref, counts_ref):
    width = cols_ref.shape[1]
    step, half = 8, peers // 2
    before = lax.broadcasted_iota(jnp.int32, (width, width), 0) < lax.broadcasted_iota(
        jnp.int32, (width, width), 1
    )
    ahead = jnp.where(before, 1.0, 0.0).astype(BF)
    first = 0 if turn_ref is None else turn_ref[0] * SLOTS
    most = jnp.zeros((peers, 128), F32)
    for k in range(4):
        total_ref[...] = jnp.zeros_like(total_ref)

        def body(g, base):
            at = pl.multiple_of(k * 32 + g * step, step)
            cols = cols_ref[pl.ds(at, step), :]
            kind = class_ref[pl.ds(pl.multiple_of(g * step, step), step), :]
            dest = cols >> 9
            lane = lax.broadcasted_iota(jnp.int32, cols.shape, 1)
            row = lax.broadcasted_iota(jnp.int32, cols.shape, 0) + g * step
            whole = (((cols >> 7) & 3) * 10 + kind, cols & 127, (lane >> 7) * 32 + row, lane & 127)
            fields = [v.astype(F32) for v in whole]
            w = weights_ref[pl.ds(at, step), :]
            w_top = w.astype(BF).astype(F32)
            fields += [w_top, w - w_top]
            for r in range(step):
                stack_ref[r * peers : (r + 1) * peers, :] = hot(peers, dest[r : r + 1])
            counts_ref[...] = jnp.dot(stack_ref[...], ahead, preferred_element_type=F32)
            for r in range(step):
                one, span = slice(r, r + 1), pl.ds(r * width, width)
                picked = stack_ref[r * peers : (r + 1) * peers, :]
                counts = counts_ref[r * peers : (r + 1) * peers, :]
                so_far = jnp.concatenate([base] * (width // 128), axis=1)
                rank = jnp.sum(picked.astype(F32) * (counts + so_far), axis=0, keepdims=True)
                last = counts[:, width - 1 :] + picked[:, width - 128 :].astype(F32)[:, 127:]
                base = base + jnp.broadcast_to(last, (peers, 128))
                slot = rank.astype(jnp.int32) - first
                kept = (slot >= 0) & (slot < SLOTS)
                slot = jnp.where(kept, slot + jnp.where(dest[one] < half, 0, SLOTS), -1)
                right_ref[:, span] = hot(2 * SLOTS, slot)
                folded_in = picked[:half] + picked[half:]
                for f, value in enumerate(fields):
                    left_ref[f * half : (f + 1) * half, span] = folded_in * value[one].astype(BF)
            total_ref[...] += lax.dot_general(left_ref[...], right_ref[...], NT, preferred_element_type=F32)
            return base

        base = lax.fori_loop(0, 32 // step, body, jnp.zeros((peers, 128), F32))
        f = [
            jnp.concatenate([total_ref[i * half : (i + 1) * half, j * SLOTS : (j + 1) * SLOTS] for j in range(2)], axis=0)
            for i in range(6)
        ]
        send_ref[:, k, :] = f[0] * 128.0 + f[1]
        cell_ref[:, k, :] = f[2] * 128.0 + f[3]
        send_ref[:, 4 + k, :] = f[4] + f[5]
        most = jnp.maximum(most, base)
    most_ref[...] = jnp.broadcast_to(jnp.max(most, keepdims=True), most_ref.shape)


def route(turn, cols, kind, weights, peers=128):
    rows, width = 4 * cols.shape[1], cols.shape[2]
    return pl.pallas_call(
        functools.partial(route_kernel, peers),
        name="route",
        out_shape=(
            jax.ShapeDtypeStruct((peers, 8, SLOTS), F32),
            jax.ShapeDtypeStruct((peers, 4, SLOTS), F32),
            jax.ShapeDtypeStruct((8, 128), F32),
        ),
        in_specs=[SM, VM, VM, VM],
        out_specs=(VM, VM, VM),
        scratch_shapes=[
            pltpu.VMEM((3 * peers, 8 * width), BF),
            pltpu.VMEM((2 * SLOTS, 8 * width), BF),
            pltpu.VMEM((3 * peers, 2 * SLOTS), F32),
            pltpu.VMEM((8 * peers, width), BF),
            pltpu.VMEM((8 * peers, width), F32),
        ],
        compiler_params=pltpu.CompilerParams(vmem_limit_bytes=48 << 20),
    )(turn, cols.reshape(rows, width), kind, weights.reshape(rows, width))


def spots(where):
    at = where.astype(jnp.int32)
    return at >> 7, at & 127


def table_terms(table, count):
    return jnp.concatenate([p.astype(F32) for p in parts(table, count)], axis=0).T.astype(BF)


def look_up(terms, rows, at):
    high = hot(rows, at >> 7)
    found = jnp.dot(terms, jnp.concatenate([high] * (terms.shape[1] // rows), axis=0), preferred_element_type=F32)
    rows = 128
    while rows > 8:
        rows //= 2
        upper = jnp.broadcast_to(at & rows, (8, at.shape[1])) > 0
        found = jnp.concatenate(
            [jnp.where(upper, found[rows + i : rows + i + 8], found[i : i + 8]) for i in range(0, rows, 8)], axis=0
        )
    return jnp.sum(jnp.where(is_row(8, at & 7), found, 0.0), axis=0, keepdims=True)


def across(pieces):
    return jnp.concatenate(pieces, axis=1)


def add_in(total_ref, values, high, low):
    both = jnp.concatenate([high * v.astype(BF) for v in values], axis=0)
    total_ref[...] += lax.dot_general(both, low, NT, preferred_element_type=F32)


GROUP = 16


def flat_rows(tiles):
    return [tiles[s, k : k + 1, :] for s in range(tiles.shape[0]) for k in range(4)]


def put_rows(out_ref, g, found):
    for s in range(GROUP):
        for k in range(4):
            i = s * 4 + k
            out_ref[g * GROUP + s, k : k + 1, :] = found[:, i * 128 : (i + 1) * 128]


def owner_group(g, got_ref, terms_ref, total_ref, back_ref):
    tile = got_ref[pl.ds(g * GROUP, GROUP), :, :]
    at_all = across(flat_rows(tile[:, :4, :].astype(jnp.int32)))
    w = across(flat_rows(tile[:, 4:, :]))
    w_top = w.astype(BF).astype(F32)
    add_in(total_ref, (w_top, w - w_top), hot(HIGH, at_all >> 7), hot(128, at_all & 127))
    put_rows(back_ref, g, look_up(terms_ref[...], 40, at_all))


def gather_group(g, terms_ref, where_ref, out_ref):
    at_all = across(flat_rows(where_ref[pl.ds(g * GROUP, GROUP), :, :].astype(jnp.int32)))
    put_rows(out_ref, g, look_up(terms_ref[...], HIGH, at_all))


def scatter_group(g, where_ref, weights_ref, values_ref, total_ref):
    span = pl.ds(g * GROUP, GROUP)
    at_all = across(flat_rows(where_ref[span, :4, :].astype(jnp.int32)))
    v = across(flat_rows(weights_ref[span, 4:, :] * values_ref[span, :, :]))
    v_top = v.astype(BF).astype(F32)
    add_in(total_ref, (v_top, v - v_top), hot(HIGH, at_all >> 7), hot(128, at_all & 127))


def owner_kernel(table_ref, got_ref, denom_ref, back_ref, terms_ref, total_ref):
    terms_ref[...] = table_terms(table_ref[...], 3)
    total_ref[...] = jnp.zeros_like(total_ref)

    @pl.loop(0, got_ref.shape[0] // GROUP)
    def _(g):
        owner_group(g, got_ref, terms_ref, total_ref, back_ref)

    denom_ref[...] = total_ref[:HIGH, :] + total_ref[HIGH:, :]


def owner(table, got):
    peers = got.shape[0]
    return pl.pallas_call(
        owner_kernel,
        name="owner",
        out_shape=(jax.ShapeDtypeStruct((HIGH, 128), F32), jax.ShapeDtypeStruct((peers, 4, SLOTS), F32)),
        in_specs=[VM, VM],
        out_specs=(VM, VM),
        scratch_shapes=[pltpu.VMEM((128, 120), BF), pltpu.VMEM((2 * HIGH, 128), F32)],
        compiler_params=pltpu.CompilerParams(vmem_limit_bytes=48 << 20),
    )(table, got)


def gather_kernel(table_ref, where_ref, out_ref, terms_ref):
    terms_ref[...] = table_terms(table_ref[...], 2)

    @pl.loop(0, where_ref.shape[0] // GROUP)
    def _(g):
        gather_group(g, terms_ref, where_ref, out_ref)


def gather(table, where):
    return pl.pallas_call(
        gather_kernel,
        name="pick",
        out_shape=jax.ShapeDtypeStruct(where.shape, F32),
        in_specs=[VM, VM],
        out_specs=VM,
        scratch_shapes=[pltpu.VMEM((128, 128), BF)],
        compiler_params=pltpu.CompilerParams(vmem_limit_bytes=48 << 20),
    )(table, where)


def scatter_kernel(where_ref, weights_ref, values_ref, out_ref, total_ref):
    total_ref[...] = jnp.zeros_like(total_ref)

    @pl.loop(0, where_ref.shape[0] // GROUP)
    def _(g):
        scatter_group(g, where_ref, weights_ref, values_ref, total_ref)

    out_ref[...] = total_ref[:HIGH, :] + total_ref[HIGH:, :]


def scatter(where, weights, values):
    return pl.pallas_call(
        scatter_kernel,
        name="put",
        out_shape=jax.ShapeDtypeStruct((HIGH, 128), F32),
        in_specs=[VM, VM, VM],
        out_specs=VM,
        scratch_shapes=[pltpu.VMEM((2 * HIGH, 128), F32)],
        compiler_params=pltpu.CompilerParams(vmem_limit_bytes=48 << 20),
    )(where, weights, values)


def place():
    wide = lax.axis_size("tx")
    return lax.axis_index("ty") * wide + lax.axis_index("tx"), lax.axis_size("ty") * wide


def at(peer):
    wide = lax.axis_size("tx")
    return (peer // wide, peer % wide)


def meet(me, peers):
    barrier = pltpu.get_barrier_semaphore()

    @pl.loop(1, peers)
    def _(step):
        pl.semaphore_signal(barrier, inc=1, device_id=at((me + step) % peers), device_id_type=MESH)

    pl.semaphore_wait(barrier, peers - 1)


def exchange_kernel(send_ref, got_ref, out_sem, in_sem, own_sem):
    me, peers = place()
    own = pltpu.make_async_copy(send_ref.at[me], got_ref.at[me], own_sem)
    own.start()
    meet(me, peers)

    @pl.loop(1, peers)
    def _(step):
        peer = (me + step) % peers
        pltpu.make_async_remote_copy(
            send_ref.at[peer], got_ref.at[me], out_sem, in_sem, device_id=at(peer), device_id_type=MESH
        ).start()

    own.wait()
    others = pl.ds(0, peers - 1)
    whole = pltpu.make_async_remote_copy(
        send_ref.at[others], got_ref.at[others], out_sem, in_sem, device_id=at((me + 1) % peers), device_id_type=MESH
    )
    whole.wait()


def exchange(send, name, number):
    return pl.pallas_call(
        exchange_kernel,
        name=name,
        out_shape=jax.ShapeDtypeStruct(send.shape, send.dtype),
        in_specs=[VM],
        out_specs=VM,
        scratch_shapes=[pltpu.SemaphoreType.DMA] * 3,
        compiler_params=pltpu.CompilerParams(collective_id=number, has_side_effects=True),
    )(send)


LEV = 10
ROWS, COLS = 32, 256
TALL, LONG = 48, 384
RIM = 8
PLANES = 3 * LEV + 4
MASK, THICK, BED, BETA = range(3 * LEV, PLANES)
PACKS = 3
ALL_ROWS = pl.ds(0, ROWS)


def pack_halo(fields, all_ref, left_ref, right_ref, each):
    vel_ref, stiff_ref, mask_ref, thick_ref, bed_ref, beta_ref = fields
    lane = lax.broadcasted_iota(jnp.int32, (ROWS, 128), 1)
    left = [jnp.zeros((ROWS, 128), F32)] * PACKS
    right = [jnp.zeros((ROWS, 128), F32)] * PACKS
    for p in range(PLANES):
        if p < 2 * LEV:
            plane = vel_ref[p]
        elif p < 3 * LEV:
            plane = stiff_ref[p - 2 * LEV]
        elif p == MASK:
            plane = mask_ref[...].astype(F32)
        else:
            plane = {THICK: thick_ref, BED: bed_ref, BETA: beta_ref}[p][...]
        all_ref[p, :ROWS, :COLS] = plane
        pack, k = p // 16, p % 16
        here = (lane >= RIM * k) & (lane < RIM * (k + 1))
        first, last = plane[:, :128], plane[:, COLS - 128 :]
        left[pack] = jnp.where(here, pltpu.roll(first, RIM * k, 1) if k else first, left[pack])
        turn = (RIM * k + RIM) % 128
        right[pack] = jnp.where(here, pltpu.roll(last, turn, 1) if turn else last, right[pack])
        each(p)
    for i in range(PACKS):
        left_ref[i] = left[i]
        right_ref[i] = right[i]


def halo_copies(all_ref, left_ref, right_ref, from_right, from_left, out_sem, in_sem):
    y, x = lax.axis_index("ty"), lax.axis_index("tx")
    tall, wide = lax.axis_size("ty"), lax.axis_size("tx")
    around = [(a, b) for a in (-1, 0, 1) for b in (-1, 0, 1) if (a, b) != (0, 0)]
    copies = []
    for i, (a, b) in enumerate(around):
        rows = {-1: pl.ds(0, RIM), 0: ALL_ROWS, 1: pl.ds(ROWS - RIM, RIM)}[a]
        there = {-1: pl.ds(ROWS, RIM), 0: ALL_ROWS, 1: pl.ds(TALL - RIM, RIM)}[a]
        if b == 0:
            ends = all_ref.at[:, rows, pl.ds(0, COLS)], all_ref.at[:, there, pl.ds(0, COLS)]
        elif b < 0:
            ends = left_ref.at[:, rows, :], from_right.at[:, there, :]
        else:
            ends = right_ref.at[:, rows, :], from_left.at[:, there, :]
        device = ((y + a + tall) % tall, (x + b + wide) % wide)
        copies.append(
            pltpu.make_async_remote_copy(
                *ends, out_sem.at[i], in_sem.at[i], device_id=device, device_id_type=MESH
            )
        )
    return copies


def unpack_halo(all_ref, from_right, from_left):
    y, x = lax.axis_index("ty"), lax.axis_index("tx")
    tall, wide = lax.axis_size("ty"), lax.axis_size("tx")
    row = lax.broadcasted_iota(jnp.int32, (TALL, 128), 0)
    lane = lax.broadcasted_iota(jnp.int32, (TALL, 128), 1)
    inside = (row < ROWS) | ((row < ROWS + RIM) & (y < tall - 1)) | ((row >= TALL - RIM) & (y > 0))
    on_right = inside & (lane < RIM) & (x < wide - 1)
    on_left = inside & (lane >= 128 - RIM) & (x > 0)
    rights = [from_right[i] for i in range(PACKS)]
    lefts = [from_left[i] for i in range(PACKS)]
    for p in range(PLANES):
        pack, k = p // 16, p % 16
        to_right = pltpu.roll(rights[pack], 128 - RIM * k, 1) if k else rights[pack]
        turn = (128 - RIM - RIM * k) % 128
        to_left = pltpu.roll(lefts[pack], turn, 1) if turn else lefts[pack]
        all_ref[p, :, COLS:] = jnp.where(on_right, to_right, jnp.where(on_left, to_left, 0.0))

    @pl.when(y == tall - 1)
    def _():
        all_ref[:, ROWS : ROWS + RIM, :COLS] = jnp.zeros((PLANES, RIM, COLS), F32)

    @pl.when(y == 0)
    def _():
        all_ref[:, TALL - RIM :, :COLS] = jnp.zeros((PLANES, RIM, COLS), F32)


def next_row(a):
    return pltpu.roll(a, a.shape[0] - 1, 0)


def last_row(a):
    return pltpu.roll(a, 1, 0)


def next_col(a):
    return pltpu.roll(a, a.shape[1] - 1, 1)


def last_col(a):
    return pltpu.roll(a, 1, 1)


def folded(a, b):
    inner = a[:ROWS, :COLS] * b[:ROWS, :COLS]
    return inner[0:8] + inner[8:16] + inner[16:24] + inner[24:32]


def apply_level(source, level, gx_ref, gy_ref, gz_ref, mask, friction):
    gx, gy = gx_ref[level], gy_ref[level]
    over, under = gz_ref[level + 1], gz_ref[level]
    upper = jnp.minimum(level + 1, LEV - 1)
    lower = jnp.maximum(level - 1, 0)
    results = []
    for c, (along_x, along_y) in enumerate(((2.0, 0.5), (0.5, 2.0))):
        w = source(c, level)
        held = mask * w
        flow_x = gx * (held - next_row(held))
        flow_y = gy * (held - next_col(held))
        value = along_x * (flow_x - last_row(flow_x)) + along_y * (flow_y - last_col(flow_y))
        value = value + over * (held - mask * source(c, upper)) + under * (held - mask * source(c, lower))
        value = value + friction * held
        results.append(jnp.where(mask > 0.0, value, w))
    return results


def planes_of(ref):
    return lambda c, level: ref[c * LEV + level]


def tile_of(pairs, last=None):
    lane = lax.broadcasted_iota(jnp.int32, (1, 128), 1)
    rows = [jnp.where(lane < 64, a, b) for a, b in pairs]
    rows += [jnp.zeros((1, 128), F32)] * (7 - len(rows))
    rows.append(jnp.zeros((1, 128), F32) if last is None else last)
    return jnp.concatenate(rows, axis=0)


def summed(sums_ref, count):
    return [jnp.sum(sums_ref[i], keepdims=True) for i in range(count)]


def begin(each, all_ref, most_ref, r0_ref, v1_ref, v2_ref, gx_ref, gy_ref, gz_ref, part_ref, mu_ref, sums_ref):
    sums_ref[...] = jnp.zeros_like(sums_ref)
    mask = all_ref[MASK]
    beta = all_ref[BETA]

    @pl.loop(0, LEV)
    def _(level):
        each(level)
        upper = jnp.minimum(level + 1, LEV - 1)
        u, v = all_ref[level], all_ref[LEV + level]
        grad_xx = 0.5 * (next_row(u) - last_row(u))
        grad_yy = 0.5 * (next_col(v) - last_col(v))
        cross = 0.5 * (next_col(u) - last_col(u)) + 0.5 * (next_row(v) - last_row(v))
        shear_x = all_ref[upper] - u
        shear_y = all_ref[LEV + upper] - v
        rate = grad_xx * grad_xx + grad_yy * grad_yy + grad_xx * grad_yy
        rate = rate + 0.25 * (cross * cross) + 0.25 * (shear_x * shear_x + shear_y * shear_y)
        base = rate + 0.1
        root = jnp.exp(jnp.log(base) * (-1.0 / 3.0))
        root = root * (4.0 - base * (root * root * root)) * (1.0 / 3.0)
        mu_ref[level] = all_ref[2 * LEV + level] * root

    gz_ref[0] = jnp.zeros((TALL, LONG), F32)
    gz_ref[LEV] = jnp.zeros((TALL, LONG), F32)

    @pl.loop(0, LEV)
    def _(level):
        mu = mu_ref[level]
        gx_ref[level] = mu + next_row(mu)
        gy_ref[level] = mu + next_col(mu)

    @pl.loop(1, LEV)
    def _(level):
        gz_ref[level] = mu_ref[level - 1] + mu_ref[level]

    s0 = all_ref[BED] + all_ref[THICK]
    force = -(mask * all_ref[THICK])
    drive = (force * (0.5 * (next_row(s0) - last_row(s0))), force * (0.5 * (next_col(s0) - last_col(s0))))

    def at_level(level):
        return jnp.where(level == 0, beta, 0.0)

    @pl.loop(0, LEV)
    def _(level):
        for c, value in enumerate(apply_level(planes_of(all_ref), level, gx_ref, gy_ref, gz_ref, mask, at_level(level))):
            r = drive[c] - value
            r0_ref[c * LEV + level] = r
            sums_ref[0] += folded(r, r)

    @pl.loop(0, LEV)
    def _(level):
        for c, value in enumerate(apply_level(planes_of(r0_ref), level, gx_ref, gy_ref, gz_ref, mask, at_level(level))):
            v1_ref[c * LEV + level] = value
            sums_ref[1] += folded(value, r0_ref[c * LEV + level])
            sums_ref[2] += folded(value, value)

    @pl.loop(0, LEV)
    def _(level):
        for c, value in enumerate(apply_level(planes_of(v1_ref), level, gx_ref, gy_ref, gz_ref, mask, at_level(level))):
            v2_ref[c * LEV + level] = value
            sums_ref[3] += folded(value, v1_ref[c * LEV + level])

    part_ref[...] = tile_of([(s, s) for s in summed(sums_ref, 4)], most_ref[:1, :])


def first_scalars(total_ref):
    m0, m1, m2, m3 = (total_ref[i : i + 1, 0:1] for i in range(4))
    a0 = m0 / m1
    rr1 = a0 * a0 * m2 - m0
    b1 = rr1 / m0
    c = 1.0 + b1
    along = c * c * m1 - 2.0 * c * a0 * m2 + a0 * a0 * m3
    a1 = rr1 / along
    return a0, a1, c, rr1, along


def middle(total_ref, all_ref, r0_ref, v1_ref, v2_ref, gx_ref, gy_ref, gz_ref, s_ref, part_ref, r2_ref, q1_ref, sums_ref):
    a0, a1, c, _, _ = first_scalars(total_ref)
    sums_ref[...] = jnp.zeros_like(sums_ref)
    mask = all_ref[MASK]
    beta = all_ref[BETA]

    @pl.loop(0, 2 * LEV)
    def _(p):
        v1 = v1_ref[p]
        q1 = c * v1 - a0 * v2_ref[p]
        r2 = r0_ref[p] - a0 * v1 - a1 * q1
        q1_ref[p] = q1
        r2_ref[p] = r2
        sums_ref[0] += folded(r2, r2)
        sums_ref[1] += folded(r2, q1)
        sums_ref[2] += folded(q1, q1)

    def at_level(level):
        return jnp.where(level == 0, beta, 0.0)

    @pl.loop(0, LEV)
    def _(level):
        for c, value in enumerate(apply_level(planes_of(r2_ref), level, gx_ref, gy_ref, gz_ref, mask, at_level(level))):
            p = c * LEV + level
            s_ref[p] = value
            sums_ref[3] += folded(value, r2_ref[p])
            sums_ref[4] += folded(value, value)
            sums_ref[5] += folded(value, q1_ref[p])

    @pl.loop(0, LEV)
    def _(level):
        for c, value in enumerate(apply_level(planes_of(q1_ref), level, gx_ref, gy_ref, gz_ref, mask, at_level(level))):
            sums_ref[6] += folded(value, q1_ref[c * LEV + level])

    @pl.loop(0, LEV)
    def _(level):
        for c, value in enumerate(apply_level(planes_of(s_ref), level, gx_ref, gy_ref, gz_ref, mask, at_level(level))):
            p = c * LEV + level
            sums_ref[7] += folded(value, s_ref[p])
            sums_ref[8] += folded(value, q1_ref[p])

    d = summed(sums_ref, 9)
    part_ref[...] = tile_of([(d[0], d[1]), (d[2], d[3]), (d[4], d[5]), (d[6], d[7]), (d[8], d[8])])


def end(first_ref, second_ref, all_ref, r0_ref, v1_ref, v2_ref, s_ref, velocity_ref):
    a0, a1, c, rr1, pq = first_scalars(first_ref)
    pair = lambda i: (second_ref[i : i + 1, 0:1], second_ref[i : i + 1, 64:65])
    (rr2, rq), (qq, rs), (ss, sq), (tq, su), (uq, _) = (pair(i) for i in range(5))
    b = rr2 / rr1
    p2q2 = rs + 2.0 * b * rq + b * b * pq
    a2 = rr2 / p2q2
    r2q2 = rs + b * rq
    q2q2 = ss + 2.0 * b * sq + b * b * qq
    rr3 = rr2 - 2.0 * a2 * r2q2 + a2 * a2 * q2q2
    b3 = rr3 / rr2
    q2t2 = su + 2.0 * b * uq + b * b * tq
    p3q3 = (
        rs
        - 2.0 * a2 * (ss + b * sq)
        + a2 * a2 * q2t2
        + 2.0 * b3 * (r2q2 - a2 * q2q2)
        + b3 * b3 * p2q2
    )
    a3 = rr3 / p3q3
    of_p2 = a2 + a3 * b3
    of_r2 = of_p2 + a3
    of_p1 = of_p2 * b + a1
    of_s = -(a3 * a2)
    of_q1 = of_s * b - of_r2 * a1
    of_r0 = a0 + of_p1 * c + of_r2
    of_v1 = of_q1 * c - of_p1 * a0 - of_r2 * a0
    of_v2 = -(of_q1 * a0)

    means = []
    for k in range(2):
        mean = jnp.zeros((TALL, LONG), F32)
        for level in range(LEV):
            p = k * LEV + level
            value = all_ref[p] + of_r0 * r0_ref[p] + of_v1 * v1_ref[p] + of_v2 * v2_ref[p] + of_s * s_ref[p]
            velocity_ref[p] = value[:ROWS, :COLS]
            mean = mean + value
        means.append(all_ref[THICK] * (mean * (1.0 / LEV)))
    spread = 0.5 * (next_row(means[0]) - last_row(means[0])) + 0.5 * (next_col(means[1]) - last_col(means[1]))
    return spread[:ROWS, :COLS]


def joined(tiles):
    row = lax.broadcasted_iota(jnp.int32, tiles.shape[1:], 0)
    return jnp.where(row < 7, jnp.sum(tiles, axis=0), jnp.max(tiles, axis=0))


class Total:
    def __init__(self, part_ref, near_ref, half_ref, far_ref, sems):
        y, x = lax.axis_index("ty"), lax.axis_index("tx")
        tall, wide = lax.axis_size("ty"), lax.axis_size("tx")
        core, chip = x % 2, x // 2
        near, far = tall * 2, wide // 2
        self.me, self.chip = y * 2 + core, chip
        ids = [(self.me + i) % near for i in range(1, near)]
        self.near_devices = [(i // 2, chip * 2 + i % 2) for i in ids]
        self.far_devices = [(y, ((chip + i) % far) * 2 + core) for i in range(1, far)]
        self.part, self.near, self.half, self.far, self.sems = part_ref, near_ref, half_ref, far_ref, sems

    def send(self, source, target, place, devices, first):
        for device in devices:
            pltpu.make_async_remote_copy(
                source, target.at[place], self.sems.at[first], self.sems.at[first + 1],
                device_id=device, device_id_type=MESH,
            ).start()
        target[pl.ds(place, 1)] = source[...][None]

    def wait(self, target, devices, first):
        whole = pl.ds(0, len(devices))
        pltpu.make_async_remote_copy(
            target.at[whole], target.at[whole], self.sems.at[first], self.sems.at[first + 1],
            device_id=devices[0], device_id_type=MESH,
        ).wait()

    def start(self):
        self.send(self.part, self.near, self.me, self.near_devices, 0)

    def turn(self):
        self.wait(self.near, self.near_devices, 0)
        self.half[...] = joined(self.near[...])
        self.send(self.half, self.far, self.chip, self.far_devices, 2)

    def finish(self, sum_ref):
        self.wait(self.far, self.far_devices, 2)
        sum_ref[...] = joined(self.far[...])


def send_block(source, target, peer, me, sems):
    pltpu.make_async_remote_copy(
        source.at[peer], target.at[me], sems.at[0], sems.at[1], device_id=at(peer), device_id_type=MESH
    ).start()


def await_blocks(source, target, me, peers, sems):
    target[pl.ds(me, 1)] = source[pl.ds(me, 1)]
    others = pl.ds(0, peers - 1)
    pltpu.make_async_remote_copy(
        source.at[others], target.at[others], sems.at[0], sems.at[1],
        device_id=at((me + 1) % peers), device_id_type=MESH,
    ).wait()


def send_group(source, target, g, me, sems):
    for s in range(GROUP):
        peer = g * GROUP + s

        @pl.when(peer != me)
        def _():
            send_block(source, target, peer, me, sems)


def whole_kernel(
    vel_ref, stiff_ref, mask_ref, thick_ref, bed_ref, beta_ref, table_ref, cols_ref, class_ref, weights_ref,
    velocity_ref, surface_ref, land_ref, spread_ref, fullest_ref,
    first_ref, all_ref, left_ref, right_ref, from_right, from_left,
    send_ref, cell_ref, most_ref, route_left, route_right, route_total, route_stack, route_counts,
    got_ref, found_ref, back_ref, value_ref, last_ref,
    r0_ref, v1_ref, v2_ref, r2_ref, q1_ref, s_ref, gx_ref, gy_ref, gz_ref, mu_ref,
    sums_ref, part1_ref, near1_ref, half1_ref, far1_ref, part2_ref, near2_ref, half2_ref, far2_ref, second_ref,
    terms_ref, surface_terms, denom_ref, smb_ref, numer_ref,
    halo_out, halo_in, total1_sem, total2_sem, to_owner, from_owner, to_land,
):
    me, peers = place()
    groups = peers // GROUP
    barrier = pltpu.get_barrier_semaphore()

    def greet(p):
        for step in range(4 * p + 1, min(4 * p + 5, 128)):
            pl.semaphore_signal(barrier, inc=1, device_id=at((me + step) % peers), device_id_type=MESH)

    pack_halo((vel_ref, stiff_ref, mask_ref, thick_ref, bed_ref, beta_ref), all_ref, left_ref, right_ref, greet)
    pl.semaphore_wait(barrier, peers - 1)
    halo = halo_copies(all_ref, left_ref, right_ref, from_right, from_left, halo_out, halo_in)
    for copy in halo:
        copy.start()
    route_kernel(
        peers, None, cols_ref, class_ref, weights_ref, send_ref, cell_ref, most_ref, route_left, route_right, route_total,
        route_stack, route_counts,
    )
    for copy in halo:
        copy.wait()
    unpack_halo(all_ref, from_right, from_left)

    def to_owners(level):
        for i in range(13):
            step = level * 13 + i + 1

            @pl.when(step < peers)
            def _():
                send_block(send_ref, got_ref, (me + step) % peers, me, to_owner)

    begin(to_owners, all_ref, most_ref, r0_ref, v1_ref, v2_ref, gx_ref, gy_ref, gz_ref, part1_ref, mu_ref, sums_ref)
    total1 = Total(part1_ref, near1_ref, half1_ref, far1_ref, total1_sem)
    total1.start()
    await_blocks(send_ref, got_ref, me, peers, to_owner)
    table = jnp.concatenate([table_ref[:, t * 128 : (t + 1) * 128] for t in range(4)], axis=0)
    terms_ref[...] = table_terms(table, 3)
    denom_ref[...] = jnp.zeros_like(denom_ref)

    def own_group(g):
        @pl.when(g > 0)
        def _():
            send_group(found_ref, back_ref, g - 1, me, from_owner)

        owner_group(g, got_ref, terms_ref, denom_ref, found_ref)

    pl.loop(0, groups // 2)(own_group)
    total1.turn()
    pl.loop(groups // 2, groups)(own_group)
    total1.finish(first_ref)
    fullest_ref[0, 0] = jnp.max(first_ref[7:8, :])
    send_group(found_ref, back_ref, groups - 1, me, from_owner)
    middle(first_ref, all_ref, r0_ref, v1_ref, v2_ref, gx_ref, gy_ref, gz_ref, s_ref, part2_ref, r2_ref, q1_ref, sums_ref)
    total2 = Total(part2_ref, near2_ref, half2_ref, far2_ref, total2_sem)
    total2.start()
    await_blocks(found_ref, back_ref, me, peers, from_owner)
    smb_ref[...] = jnp.zeros_like(smb_ref)

    def cell_group(g):
        scatter_group(g, cell_ref, send_ref, back_ref, smb_ref)

    pl.loop(0, groups // 2)(cell_group)
    total2.turn()
    pl.loop(groups // 2, groups)(cell_group)
    total2.finish(second_ref)
    spread = end(first_ref, second_ref, all_ref, r0_ref, v1_ref, v2_ref, s_ref, velocity_ref)
    spread_ref[...] = spread
    smb = smb_ref[:HIGH, :] + smb_ref[HIGH:, :]
    halves = []
    for h in range(2):
        side = slice(h * 128, (h + 1) * 128)
        half = bed_ref[:, side] + thick_ref[:, side] + 0.5 * (smb[h * ROWS : (h + 1) * ROWS] - spread[:, side])
        surface_ref[:, side] = half
        halves.append(half)
    surface_terms[...] = table_terms(jnp.concatenate(halves, axis=0), 2)

    @pl.loop(0, groups)
    def _(g):
        @pl.when(g > 0)
        def _():
            send_group(value_ref, last_ref, g - 1, me, to_land)

        gather_group(g, surface_terms, cell_ref, value_ref)

    numer_ref[...] = jnp.zeros_like(numer_ref)
    send_group(value_ref, last_ref, groups - 1, me, to_land)
    await_blocks(value_ref, last_ref, me, peers, to_land)

    @pl.loop(0, groups)
    def _(g):
        scatter_group(g, got_ref, got_ref, last_ref, numer_ref)

    classes = land_ref.shape[0]
    for t in range(4):
        numer, denom = (
            ref[t * classes : (t + 1) * classes, :] + ref[HIGH + t * classes : HIGH + (t + 1) * classes, :]
            for ref in (numer_ref, denom_ref)
        )
        land_ref[:, t * 128 : (t + 1) * 128] = numer / (denom + 1.0)


def whole(velocity, stiffness, mask, thickness, bed, beta, table, cols, kind, weights):
    tall, wide = lax.axis_size("ty"), lax.axis_size("tx")
    peers = tall * wide
    shape = lambda *dims: jax.ShapeDtypeStruct(dims, F32)
    room = lambda *dims: pltpu.VMEM(dims, F32)
    block, level = (2 * LEV, TALL, LONG), (LEV, TALL, LONG)
    sum_room = [room(8, 128), room(2 * tall, 8, 128), room(8, 128), room(wide // 2, 8, 128)]
    pair = pltpu.SemaphoreType.DMA((2,))
    return pl.pallas_call(
        whole_kernel,
        name="whole",
        out_shape=(shape(2 * LEV, ROWS, COLS), shape(ROWS, COLS), shape(*table.shape), shape(ROWS, COLS), shape(1, 1)),
        in_specs=[VM] * 10,
        out_specs=(VM,) * 4 + (SM,),
        scratch_shapes=[
            room(8, 128),
            room(PLANES, TALL, LONG), room(PACKS, ROWS, 128), room(PACKS, ROWS, 128),
            room(PACKS, TALL, 128), room(PACKS, TALL, 128),
            room(peers, 8, SLOTS), room(peers, 4, SLOTS), room(8, 128),
            pltpu.VMEM((3 * peers, 8 * COLS), BF), pltpu.VMEM((2 * SLOTS, 8 * COLS), BF), room(3 * peers, 2 * SLOTS),
            pltpu.VMEM((8 * peers, COLS), BF), room(8 * peers, COLS),
            room(peers, 8, SLOTS), room(peers, 4, SLOTS), room(peers, 4, SLOTS), room(peers, 4, SLOTS), room(peers, 4, SLOTS),
            room(*block), room(*block), room(*block), room(*block), room(*block), room(*block),
            room(*level), room(*level), room(LEV + 1, TALL, LONG), room(*level),
            room(9, 8, COLS), *sum_room, *sum_room, room(8, 128),
            pltpu.VMEM((128, 120), BF), pltpu.VMEM((128, 128), BF),
            room(2 * HIGH, 128), room(2 * HIGH, 128), room(2 * HIGH, 128),
            pltpu.SemaphoreType.DMA((8,)), pltpu.SemaphoreType.DMA((8,)),
            pltpu.SemaphoreType.DMA((4,)), pltpu.SemaphoreType.DMA((4,)), pair, pair, pair,
        ],
        compiler_params=pltpu.CompilerParams(
            collective_id=1, has_side_effects=True, vmem_limit_bytes=60 << 20
        ),
    )(
        velocity.reshape(2 * LEV, ROWS, COLS), stiffness, mask, thickness, bed, beta, table,
        cols.reshape(4 * ROWS, COLS), kind, weights.reshape(4 * ROWS, COLS),
    )


def on_device(
    velocity_start,
    stiffness,
    beta,
    ice_mask,
    thickness,
    bed,
    land_smb,
    elev_class,
    correlation_cols,
    correlation_weights,
):
    velocity, surface, land, spread, fullest = whole(
        velocity_start, stiffness, ice_mask, thickness, bed, beta, land_smb, correlation_cols, elev_class, correlation_weights
    )
    turns = ((fullest[0, 0].astype(jnp.int32) + SLOTS - 1) // SLOTS).astype(jnp.int32)


    def turn(number):
        return route(
            jnp.full((1,), number, jnp.int32), correlation_cols, elev_class, correlation_weights
        )

    def unfinished(carry):
        return carry[0] < turns

    table = jnp.concatenate([land_smb[:, t * 128 : (t + 1) * 128] for t in range(4)], axis=0)
    again = turns > 1
    start = jnp.where(again, 0, turns)

    def balance(carry):
        number, smb, denom = carry
        send, cell, _ = turn(number)
        add_denom, found = owner(table, exchange(send, "more_to_owner", 2))
        return number + 1, smb + scatter(cell, send, exchange(found, "more_from_owner", 3)), denom + add_denom

    none = jnp.zeros((HIGH, 128), F32)
    _, smb, denom = lax.while_loop(unfinished, balance, (start, none, none))
    halves = [
        bed[:, s] + thickness[:, s] + 0.5 * (smb[h * ROWS : (h + 1) * ROWS] - spread[:, s])
        for h, s in enumerate((slice(0, 128), slice(128, 256)))
    ]
    rows = jnp.concatenate(halves, axis=0)

    def raised(carry):
        number, numer = carry
        send, cell, _ = turn(number)
        got = exchange(send, "again_to_owner", 4)
        return number + 1, numer + scatter(got, got, exchange(gather(rows, cell), "again_to_land", 5))

    _, numer = lax.while_loop(unfinished, raised, (start, none))
    ratio, classes = numer / (denom + 1.0), land_smb.shape[0]
    land_again = jnp.concatenate([ratio[t * classes : (t + 1) * classes] for t in range(4)], axis=1)
    surface = jnp.where(again, jnp.concatenate(halves, axis=1), surface)
    land = jnp.where(again, land_again, land)
    return velocity.reshape(velocity_start.shape), surface, land


def solution(mesh):
    every = ("ty", "tx")
    return jax.shard_map(
        on_device,
        mesh=mesh,
        in_specs=(
            P(None, None, "ty", "tx"),
            P(None, "ty", "tx"),
            P("ty", "tx"),
            P("ty", "tx"),
            P("ty", "tx"),
            P("ty", "tx"),
            P(None, every),
            P("ty", "tx"),
            P(None, "ty", "tx"),
            P(None, "ty", "tx"),
        ),
        out_specs=(P(None, None, "ty", "tx"), P("ty", "tx"), P(None, every)),
        check_vma=False,
    )
```
